32 devices in a mesh: dp: 4 (over y, x), ctx: 8 (over z, core).
Axes of the slice: x: 2, y: 2, z: 4, core: 2. Of those that a mesh axis runs over, the one named last changes fastest.
Arguments:
- queries: bfloat16 [2048, 2048], P(('dp', 'ctx')), parts along dimension 0, may hold values from -10 to 10
- keys: bfloat16 [2048, 512], P(('dp', 'ctx')), parts along dimension 0, may hold values from -10 to 10
- values: bfloat16 [2048, 512], P(('dp', 'ctx')), parts along dimension 0, may hold values from -6 to 6
- block_order: int32 [64], P(('dp', 'ctx')), parts along dimension 0, may hold values from 0 to 15, as said below
- doc_lengths: int32 [16], P('dp'), parts along dimension 0, may hold values from 1 to 256, 512 in all
Outputs:
- attended: bfloat16 [2048, 2048], P(('dp', 'ctx')), parts along dimension 0
The draws below stay inside these ranges and needn't reach their ends.
There are 4 independent parts, one for each index of `dp`. The reference program is written for one: setup_inputs(seed, part) draws one part's arguments, and reference() takes and returns one part's arrays. A program takes and returns all parts, laid end to end along the dimension named above; each array names one. Nothing has to cross between parts.
Inputs may be any that keep to these rules, and one draw needn't show every extreme that they name: Storage block j (rows j * 32 to j * 32 + 31) holds the tokens of window block block_order[j]; storage blocks 2 i and 2 i + 1 hold window blocks p and 15 - p for some p, in either order; every block once. `doc_lengths`: the window's documents in order; they sum to 512.
All inputs are finite; a program needn't handle non-finite values.
Results may differ from the reference program's by a relative error of at most 0.0045.
Values may be sent and summed in bfloat16 or wider, within the bound.
No kernel may reach another device: no remote copies, remote signals or barrier semaphores. Data moves between devices by JAX's collectives and lax.ppermute only.
A program may use at most 64 MiB of HBM per device.

```python
import math
import jax
import jax.numpy as jnp
import numpy as np
from jax import lax

QH = 16
KH = 4
HD = 128
BLOCK = 32
DOCS = 4
TOK_DEV = 64
TOKENS = 512
BLOCKS = 16
MAXDOC = 256


def attention_inputs(key):
    base = jax.random.fold_in(key, 11)
    first_key, second_key = jax.random.split(base, 2)
    query_raw = jnp.clip(jax.random.normal(first_key, (TOKENS, QH * HD), jnp.float32), -4.0, 4.0)
    key_raw = jnp.clip(jax.random.normal(second_key, (TOKENS, KH * HD), jnp.float32), -4.0, 4.0)
    return (query_raw, key_raw)


def draw_queries(key, part):
    return attention_inputs(key)[0].astype(jnp.bfloat16)


def draw_keys(key, part):
    return attention_inputs(key)[1].astype(jnp.bfloat16)


def draw_block_order(key, part):
    half_count = BLOCKS // 2
    pair_key, flip_key = jax.random.split(jax.random.fold_in(key, 23))
    pairs = jax.random.permutation(pair_key, half_count).astype(jnp.int32)
    flips = jax.random.randint(flip_key, (half_count,), 0, 2, dtype=jnp.int32)
    mirror = (BLOCKS - 1 - pairs).astype(jnp.int32)
    early = jnp.where(flips == 1, mirror, pairs)
    late = jnp.where(flips == 1, pairs, mirror)
    return jnp.stack([early, late], axis=1).reshape(BLOCKS).astype(jnp.int32)


def level_of(key, extent, cuts, least, high):
    gain = 1.0
    for dim, blocks in cuts:
        steps = jax.random.uniform(jax.random.fold_in(jax.random.fold_in(key, 6), dim), (blocks,), jnp.float32, least / len(cuts), high / len(cuts))
        gain = gain * jnp.repeat(jnp.exp(steps), extent[dim] // blocks).reshape((-1,) + (1,) * (len(extent) - 1 - dim))
    return gain


def split_up(amount, total, most, slope):
    portions = [(1 << 20) // math.isqrt(rank ** slope) + 1 for rank in range(2, amount + 1)]
    rest, given = total - most - (amount - 1), [1] * (amount - 1)
    while rest > 0:
        movable = [i for i in range(amount - 1) if given[i] < most]
        pool, remaining = sum([portions[i] for i in movable]), rest
        for i in movable:
            addition = min(most - given[i], max(1, remaining * portions[i] // pool), rest)
            given[i] = given[i] + addition
            rest = rest - addition
    return np.array([most] + given)


def ragged(stream_key, number_of, total, reach, slope):
    if number_of == 2:
        one = jax.random.randint(stream_key, (), max(1, total - reach), min(reach, total - 1) + 1)
        return jnp.stack([one, total - one])
    tallies = jnp.asarray(split_up(number_of, total, reach, slope), jnp.int32)
    couples = (number_of - 1) // 2
    giver, taker = tallies[1:1 + 2 * couples:2], tallies[2:2 + 2 * couples:2]
    margin = jnp.minimum(giver - 1, reach - taker)
    passed = jax.random.randint(jax.random.fold_in(stream_key, 1), (couples,), 0, 1 << 20) % (margin + 1)
    tallies = tallies.at[1:1 + 2 * couples:2].set(giver - passed).at[2:2 + 2 * couples:2].set(taker + passed)
    return tallies[jax.random.permutation(jax.random.fold_in(stream_key, 2), number_of)]


def centred(rng, shape, width, reach, shards=(), held_as=jnp.bfloat16):
    factor_of = level_of(rng, shape, shards, -0.22, 0.18) if shards else 1.0
    values = jax.random.normal(rng, shape, jnp.float32) * width * factor_of
    return jnp.minimum(jnp.maximum(values, -reach), reach).astype(held_as)


def setup_inputs(seed: int = 0, part: int = 0) -> dict:
    splits = jax.random.split(jax.random.key(seed), 6)
    own_keys = jax.random.split(jax.random.fold_in(splits[5], part), 6)
    return {
        "queries": draw_queries(jax.random.fold_in(jax.random.fold_in(splits[5], part), 71), part),
        "keys": draw_keys(jax.random.fold_in(jax.random.fold_in(splits[5], part), 71), part),
        "values": centred(own_keys[2], (TOKENS, KH * HD), 1.0, 6.0, ((0, 8),)),
        "block_order": draw_block_order(jax.random.fold_in(jax.random.fold_in(splits[5], part), 71), part),
        "doc_lengths": ragged(own_keys[4], DOCS, TOKENS, MAXDOC, 2).astype(jnp.int32),
    }


def document_of(doc_ends, positions):
    return lax.optimization_barrier(jnp.sum((doc_ends[None, :] <= positions[:, None]).astype(jnp.int32), axis=1))

def reference(queries, keys, values, block_order, doc_lengths):
    row_ids = jnp.arange(TOKENS, dtype=jnp.int32)
    positions = (block_order[row_ids // BLOCK] * BLOCK + row_ids % BLOCK).astype(jnp.int32)
    doc_ends = jnp.cumsum(doc_lengths).astype(jnp.int32)
    documents = document_of(doc_ends, positions)
    heads_group = QH // KH
    score_scale = 1.0 / math.sqrt(HD)
    query_all = queries.astype(jnp.float32).reshape(TOKENS // TOK_DEV, TOK_DEV, KH, heads_group, HD)
    key_all = keys.astype(jnp.float32).reshape(TOKENS, KH, HD)
    value_all = values.astype(jnp.float32).reshape(TOKENS, KH, HD)
    query_pos = positions.reshape(TOKENS // TOK_DEV, TOK_DEV)
    query_doc = documents.reshape(TOKENS // TOK_DEV, TOK_DEV)

    def one_block(inputs):
        query_rows, pos_rows, doc_rows = inputs
        scores = jnp.einsum('tgjd,sgd->tgjs', query_rows, key_all) * score_scale
        allowed = (documents[None, :] == doc_rows[:, None]) & (positions[None, :] <= pos_rows[:, None])
        pair_mask = allowed[:, None, None, :]
        masked = jnp.where(pair_mask, scores, -jnp.inf)
        row_top = lax.optimization_barrier(jnp.max(masked, axis=-1, keepdims=True))
        weights = jnp.where(pair_mask, jnp.exp(masked - row_top), 0.0)
        row_total = lax.optimization_barrier(jnp.sum(weights, axis=-1))
        rounded = lax.optimization_barrier(weights.astype(jnp.bfloat16)).astype(jnp.float32)
        mixed = jnp.einsum('tgjs,sgd->tgjd', rounded, value_all) / row_total[..., None]
        return mixed.astype(jnp.bfloat16).reshape(TOK_DEV, QH * HD)
    return lax.map(one_block, (query_all, query_pos, query_doc)).reshape(TOKENS, QH * HD)
```

```python
import math
from functools import partial

import jax
import jax.numpy as jnp
from jax import lax
from jax.experimental import pallas as pl
from jax.experimental.pallas import tpu as pltpu
from jax.sharding import PartitionSpec as P

QH = 16
KH = 4
HD = 128
BLOCK = 32
GROUP = QH // KH
TAG = 8
NEGATIVE = -1e30
VMEM = pl.BlockSpec(memory_space=pltpu.VMEM)
SMEM = pl.BlockSpec(memory_space=pltpu.SMEM)


def tag_kernel(order_ref, keys_ref, out_ref):
    rows, width = keys_ref.shape
    out_ref[:rows, :] = keys_ref[...]
    lane = lax.broadcasted_iota(jnp.int32, (TAG, width), 1)
    block = jnp.where((lane // BLOCK) % 2 == 0, order_ref[0], order_ref[1])
    out_ref[rows:, :] = block.astype(jnp.float32).astype(jnp.bfloat16)


def tag_keys(block_order, keys):
    rows, width = keys.shape
    return pl.pallas_call(
        tag_kernel,
        out_shape=jax.ShapeDtypeStruct((rows + TAG, width), keys.dtype),
        in_specs=[SMEM, VMEM],
        out_specs=VMEM,
        name="tag",
    )(block_order, keys)


def weights_kernel(count, order_ref, lengths_ref, queries_ref, *refs):
    key_refs = refs[:count]
    weights_ref, total_ref, keys_all, allowed_ref = refs[count:]
    rows = queries_ref.shape[0]
    tokens = count * rows
    for index in range(count):
        keys_all[index * rows : (index + 1) * rows, :] = key_refs[index][:rows, :]

    row = lax.broadcasted_iota(jnp.int32, (rows, 128), 0)
    query_pos = jnp.where(row < BLOCK, order_ref[0], order_ref[1]) * BLOCK + row % BLOCK
    first_pos = jnp.zeros_like(query_pos)
    end = 0
    for doc in range(lengths_ref.shape[0]):
        end = end + lengths_ref[doc]
        first_pos = jnp.where(query_pos >= end, end, first_pos)
    lane = lax.broadcasted_iota(jnp.int32, (TAG, 128), 1)
    for pair in range(count // 2):
        early = key_refs[2 * pair][rows:, :128].astype(jnp.float32)
        late = key_refs[2 * pair + 1][rows:, :128].astype(jnp.float32)
        block = jnp.where(lane < rows, early, late).astype(jnp.int32)
        key_pos = (block * BLOCK + lane % BLOCK)[:1, :]
        allowed = (key_pos >= first_pos) & (key_pos <= query_pos)
        allowed_ref[:, pair * 128 : (pair + 1) * 128] = jnp.where(allowed, 0.0, NEGATIVE)

    scale = math.log2(math.e) / math.sqrt(HD)
    for head in range(KH):
        keys_head = keys_all[:, head * HD : (head + 1) * HD]
        for inner in range(GROUP):
            at = (head * GROUP + inner) * HD
            scores = lax.dot_general(
                queries_ref[:, at : at + HD],
                keys_head,
                (((1,), (1,)), ((), ())),
                preferred_element_type=jnp.float32,
            )
            masked = jnp.where(allowed_ref[...] == 0.0, scores, NEGATIVE)
            top = jnp.max(masked, axis=1, keepdims=True)
            weights = jnp.exp2((masked - top) * scale)
            rows_at = slice(inner * rows, (inner + 1) * rows)
            total_ref[head, rows_at, :] = jnp.sum(weights, axis=1, keepdims=True)
            weights_ref[head, rows_at, :] = weights.astype(jnp.bfloat16)


def attention_weights(block_order, doc_lengths, queries, key_parts):
    count = len(key_parts)
    rows = queries.shape[0]
    tokens = count * rows
    work = KH * GROUP * rows * tokens
    return pl.pallas_call(
        partial(weights_kernel, count),
        out_shape=(
            jax.ShapeDtypeStruct((KH, GROUP * rows, tokens), jnp.bfloat16),
            jax.ShapeDtypeStruct((KH, GROUP * rows, 1), jnp.float32),
        ),
        in_specs=[SMEM, SMEM, VMEM] + [VMEM] * count,
        out_specs=(VMEM, VMEM),
        scratch_shapes=[
            pltpu.VMEM((tokens, KH * HD), jnp.bfloat16),
            pltpu.VMEM((rows, tokens), jnp.float32),
        ],
        compiler_params=pltpu.CompilerParams(vmem_limit_bytes=48 << 20),
        cost_estimate=pl.CostEstimate(
            flops=2 * work * HD, transcendentals=work, bytes_accessed=2 * work
        ),
        name="weights",
    )(block_order, doc_lengths, queries, *key_parts)


def mix_kernel(count, weights_ref, total_ref, *refs):
    value_refs = refs[:count]
    out_ref, values_all = refs[count:]
    rows = value_refs[0].shape[0]
    for index in range(count):
        values_all[index * rows : (index + 1) * rows, :] = value_refs[index][...]
    for head in range(KH):
        mixed = jnp.dot(
            weights_ref[head],
            values_all[:, head * HD : (head + 1) * HD],
            preferred_element_type=jnp.float32,
        )
        mixed = (mixed / total_ref[head]).astype(jnp.bfloat16)
        for inner in range(GROUP):
            at = (head * GROUP + inner) * HD
            out_ref[:, at : at + HD] = mixed[inner * rows : (inner + 1) * rows, :]


def mix_values(weights, total, value_parts):
    count = len(value_parts)
    rows = value_parts[0].shape[0]
    tokens = count * rows
    work = KH * GROUP * rows * tokens
    return pl.pallas_call(
        partial(mix_kernel, count),
        out_shape=jax.ShapeDtypeStruct((rows, QH * HD), jnp.bfloat16),
        in_specs=[VMEM, VMEM] + [VMEM] * count,
        out_specs=VMEM,
        scratch_shapes=[pltpu.VMEM((tokens, KH * HD), jnp.bfloat16)],
        compiler_params=pltpu.CompilerParams(vmem_limit_bytes=48 << 20),
        cost_estimate=pl.CostEstimate(
            flops=2 * work * HD, transcendentals=0, bytes_accessed=2 * work
        ),
        name="mix",
    )(weights, total, *value_parts)


def on_device(devices, queries, keys, values, block_order, doc_lengths):
    chips = devices // 2
    other_core = [(i, i ^ 1) for i in range(devices)]

    def from_chip(array, step):
        pairs = [
            (2 * chip + core, 2 * ((chip + step) % chips) + core)
            for chip in range(chips)
            for core in range(2)
        ]
        return lax.ppermute(array, "ctx", pairs)

    def across(array):
        return lax.ppermute(array, "ctx", other_core)

    tagged = tag_keys(block_order, keys)
    key_parts = [tagged] + [from_chip(tagged, step) for step in range(1, chips)]
    value_parts = [values] + [from_chip(values, step) for step in range(1, chips)]
    key_parts = key_parts + [across(part) for part in key_parts]
    value_parts = value_parts + [across(part) for part in value_parts]
    weights, total = attention_weights(block_order, doc_lengths, queries, key_parts)
    return mix_values(weights, total, value_parts)


def solution(mesh):
    return jax.shard_map(
        partial(on_device, mesh.shape["ctx"]),
        mesh=mesh,
        in_specs=(
            P(("dp", "ctx"), None),
            P(("dp", "ctx"), None),
            P(("dp", "ctx"), None),
            P(("dp", "ctx")),
            P("dp"),
        ),
        out_specs=P(("dp", "ctx"), None),
        check_vma=False,
    )
```

```python
import math
from functools import partial

import jax
import jax.numpy as jnp
from jax import lax
from jax.experimental import pallas as pl
from jax.experimental.pallas import tpu as pltpu
from jax.sharding import PartitionSpec as P

QH = 16
KH = 4
HD = 128
BLOCK = 32
GROUP = QH // KH
TAG = 8
NEGATIVE = -1e30
SCALE = math.log2(math.e) / math.sqrt(HD)
VMEM = pl.BlockSpec(memory_space=pltpu.VMEM)
SMEM = pl.BlockSpec(memory_space=pltpu.SMEM)
ANY = pl.BlockSpec(memory_space=pl.ANY)


def pack_kernel(order_ref, keys_ref, values_ref, out_ref, order, sems):
    rows, width = keys_ref.shape
    copies = (
        pltpu.make_async_copy(order_ref, order, sems.at[0]),
        pltpu.make_async_copy(keys_ref, out_ref.at[pl.ds(0, rows), pl.ds(0, width)], sems.at[1]),
        pltpu.make_async_copy(values_ref, out_ref.at[pl.ds(0, rows), pl.ds(width, width)], sems.at[2]),
    )
    for copy in copies:
        copy.start()
    copies[0].wait()
    lane = lax.broadcasted_iota(jnp.int32, (TAG, 2 * width), 1)
    block = jnp.where((lane // BLOCK) % 2 == 0, order[0], order[1])
    out_ref[rows:, :] = block.astype(jnp.float32).astype(jnp.bfloat16)
    copies[1].wait()
    copies[2].wait()


def pack(block_order, keys, values):
    rows, width = keys.shape
    return pl.pallas_call(
        pack_kernel,
        out_shape=pltpu.VMEM((rows + TAG, 2 * width), keys.dtype),
        in_specs=[ANY, ANY, ANY],
        out_specs=VMEM,
        scratch_shapes=[
            pltpu.SMEM(block_order.shape, jnp.int32),
            pltpu.SemaphoreType.DMA((3,)),
        ],
        name="pack",
    )(block_order, keys, values)


def stage_kernel(count, first, last, order_ref, lengths_ref, queries_ref, *refs):
    part_refs, refs = refs[:count], refs[count:]
    if not first:
        (top_in, total_in, mixed_in), refs = refs[:3], refs[3:]
    if last:
        out_ref, staged, sems = refs
    else:
        top_out, total_out, mixed_out = refs
    rows = queries_ref.shape[0]
    width = KH * HD

    row = lax.broadcasted_iota(jnp.int32, (rows, 128), 0)
    query_pos = jnp.where(row < BLOCK, order_ref[0], order_ref[1]) * BLOCK + row % BLOCK
    first_pos = jnp.zeros_like(query_pos)
    end = 0
    for doc in range(lengths_ref.shape[0]):
        end = end + lengths_ref[doc]
        first_pos = jnp.where(query_pos >= end, end, first_pos)
    lane = lax.broadcasted_iota(jnp.int32, (TAG, 128), 1)
    masks = []
    for pair in range(count // 2):
        early = part_refs[2 * pair][rows:, :128].astype(jnp.float32)
        late = part_refs[2 * pair + 1][rows:, :128].astype(jnp.float32)
        block = jnp.where(lane < rows, early, late).astype(jnp.int32)
        key_pos = (block * BLOCK + lane % BLOCK)[:1, :]
        allowed = (key_pos >= first_pos) & (key_pos <= query_pos)
        masks.append(jnp.where(allowed, 0.0, NEGATIVE))
    mask = jnp.concatenate(masks, axis=1)
    mask = jnp.concatenate([mask] * GROUP, axis=0)

    copies = []
    for head in range(KH):
        at = head * GROUP * HD
        queries = jnp.concatenate(
            [queries_ref[:, at + g * HD : at + (g + 1) * HD] for g in range(GROUP)], axis=0
        )
        keys = jnp.concatenate(
            [part[:rows, head * HD : (head + 1) * HD] for part in part_refs], axis=0
        )
        values = jnp.concatenate(
            [part[:rows, width + head * HD : width + (head + 1) * HD] for part in part_refs],
            axis=0,
        )
        scores = lax.dot_general(
            queries, keys, (((1,), (1,)), ((), ())), preferred_element_type=jnp.float32
        )
        scores = scores + mask
        top = jnp.max(scores, axis=1, keepdims=True)
        if not first:
            before = top_in[head]
            top = jnp.maximum(top, before[:, :1])
        weights = jnp.exp2((scores - top) * SCALE)
        total = jnp.broadcast_to(jnp.sum(weights, axis=1, keepdims=True), (GROUP * rows, HD))
        mixed = jnp.dot(weights.astype(jnp.bfloat16), values, preferred_element_type=jnp.float32)
        if not first:
            factor = jnp.exp2((before - top) * SCALE)
            total = total + total_in[head] * factor
            mixed = mixed + mixed_in[head] * factor
        if last:
            mixed = (mixed * (1.0 / total)).astype(jnp.bfloat16)
            for g in range(GROUP):
                staged[:, at + g * HD : at + (g + 1) * HD] = mixed[g * rows : (g + 1) * rows, :]
            columns = pl.ds(at, GROUP * HD)
            copy = pltpu.make_async_copy(staged.at[:, columns], out_ref.at[:, columns], sems.at[head])
            copy.start()
            copies.append(copy)
        else:
            top_out[head] = jnp.broadcast_to(top, (GROUP * rows, HD))
            total_out[head] = total
            mixed_out[head] = mixed
    for copy in copies:
        copy.wait()


def attend(block_order, doc_lengths, queries, parts, state, last):
    count = len(parts)
    rows = queries.shape[0]
    work = KH * GROUP * rows * count * rows
    out_shape = (jax.ShapeDtypeStruct((KH, GROUP * rows, HD), jnp.float32),) * 3
    if last:
        out_shape = jax.ShapeDtypeStruct(queries.shape, jnp.bfloat16)
    return pl.pallas_call(
        partial(stage_kernel, count, not state, last),
        out_shape=out_shape,
        in_specs=[SMEM, SMEM, VMEM] + [VMEM] * (count + len(state)),
        out_specs=ANY if last else (VMEM, VMEM, VMEM),
        scratch_shapes=[
            pltpu.VMEM(queries.shape, jnp.bfloat16),
            pltpu.SemaphoreType.DMA((KH,)),
        ]
        if last
        else [],
        compiler_params=pltpu.CompilerParams(vmem_limit_bytes=40 << 20),
        cost_estimate=pl.CostEstimate(
            flops=4 * work * HD, transcendentals=work, bytes_accessed=4 * work
        ),
        name="last_stage" if last else "stage",
    )(block_order, doc_lengths, queries, *parts, *state)


def on_device(devices, queries, keys, values, block_order, doc_lengths):
    chips = devices // 2
    other_core = [(i, i ^ 1) for i in range(devices)]
    paired = chips & (chips - 1) == 0

    def from_chip(array, step):
        pairs = []
        for chip in range(chips):
            other = chip ^ step if paired else (chip + step) % chips
            pairs += [(2 * chip + core, 2 * other + core) for core in range(2)]
        return lax.ppermute(array, "ctx", pairs)

    def across(array):
        return lax.ppermute(array, "ctx", other_core)

    own = pack(block_order, keys, values)
    steps = STEPS if chips == 4 else range(1, chips)
    arrived = [own] + [from_chip(own, step) for step in steps]
    state = ()
    groups = GROUPS if chips == 4 else [range(at, min(at + 4, chips)) for at in range(0, chips, 4)]
    for group in groups:
        parts = [half for index in group for half in (arrived[index], across(arrived[index]))]
        state = attend(block_order, doc_lengths, queries, parts, state, group is groups[-1])
    return state


STEPS = (2, 3, 1)
GROUPS = ((0, 3), (1, 2))


def solution(mesh):
    return jax.shard_map(
        partial(on_device, mesh.shape["ctx"]),
        mesh=mesh,
        in_specs=(
            P(("dp", "ctx"), None),
            P(("dp", "ctx"), None),
            P(("dp", "ctx"), None),
            P(("dp", "ctx")),
            P("dp"),
        ),
        out_specs=P(("dp", "ctx"), None),
        check_vma=False,
    )
```

```python
import math
from functools import partial

import jax
import jax.numpy as jnp
from jax import lax
from jax.experimental import pallas as pl
from jax.experimental.pallas import tpu as pltpu
from jax.sharding import PartitionSpec as P

QH = 16
KH = 4
HD = 128
BLOCK = 32
GROUP = QH // KH
TAG = 8
NEGATIVE = -1e30
SCALE = math.log2(math.e) / math.sqrt(HD)
VMEM = pl.BlockSpec(memory_space=pltpu.VMEM)
ANY = pl.BlockSpec(memory_space=pl.ANY)


def pack_kernel(
    order_ref, lengths_ref, keys_ref, values_ref, packed_ref, span_ref, order, lengths, sems
):
    rows = keys_ref.shape[0]
    copies = [
        pltpu.make_async_copy(order_ref, order, sems.at[0]),
        pltpu.make_async_copy(lengths_ref, lengths, sems.at[1]),
    ]
    for index in range(2 * KH):
        source = keys_ref if index < KH else values_ref
        copies.append(
            pltpu.make_async_copy(
                source.at[:, pl.ds(index % KH * HD, HD)],
                packed_ref.at[pl.ds(index * rows, rows), :],
                sems.at[2 + index],
            )
        )
    for copy in copies:
        copy.start()
    copies[0].wait()
    copies[1].wait()
    lane = lax.broadcasted_iota(jnp.int32, (TAG, HD), 1)
    block = jnp.where((lane // BLOCK) % 2 == 0, order[0], order[1])
    packed_ref[2 * KH * rows :, :] = block.astype(jnp.float32).astype(jnp.bfloat16)
    row = lax.broadcasted_iota(jnp.int32, (rows, 128), 0)
    position = jnp.where(row < BLOCK, order[0], order[1]) * BLOCK + row % BLOCK
    first = jnp.zeros_like(position)
    end = 0
    for doc in range(lengths.shape[0]):
        end = end + lengths[doc]
        first = jnp.where(position >= end, end, first)
    span_ref[0] = first
    span_ref[1] = position
    for copy in copies[2:]:
        copy.wait()


def pack(block_order, doc_lengths, keys, values):
    rows = keys.shape[0]
    return pl.pallas_call(
        pack_kernel,
        out_shape=(
            pltpu.VMEM((2 * KH * rows + TAG, HD), keys.dtype),
            pltpu.VMEM((2, rows, 128), jnp.int32),
        ),
        in_specs=[ANY, ANY, ANY, ANY],
        out_specs=(VMEM, VMEM),
        scratch_shapes=[
            pltpu.SMEM(block_order.shape, jnp.int32),
            pltpu.SMEM(doc_lengths.shape, jnp.int32),
            pltpu.SemaphoreType.DMA((2 + 2 * KH,)),
        ],
        name="pack",
    )(block_order, doc_lengths, keys, values)


def fetch_kernel(queries_ref, out_ref, sem):
    copy = pltpu.make_async_copy(queries_ref, out_ref, sem)
    copy.start()
    copy.wait()


def fetch(queries):
    return pl.pallas_call(
        fetch_kernel,
        out_shape=pltpu.VMEM(queries.shape, queries.dtype),
        in_specs=[ANY],
        out_specs=VMEM,
        scratch_shapes=[pltpu.SemaphoreType.DMA],
        cost_estimate=pl.CostEstimate(
            flops=0, transcendentals=0, bytes_accessed=16 * queries.size
        ),
        name="fetch",
    )(queries)


def attend_kernel(count, span_ref, queries_ref, *refs):
    part_refs = refs[:count]
    out_ref, staged, sems = refs[count:]
    rows = queries_ref.shape[0]
    columns = GROUP * HD

    lane = lax.broadcasted_iota(jnp.int32, (TAG, 128), 1)
    masks = []
    for pair in range(count // 2):
        early = part_refs[2 * pair][2 * KH * rows :, :].astype(jnp.float32)
        late = part_refs[2 * pair + 1][2 * KH * rows :, :].astype(jnp.float32)
        block = jnp.where(lane < rows, early, late).astype(jnp.int32)
        position = (block * BLOCK + lane % BLOCK)[:1, :]
        allowed = (position >= span_ref[0]) & (position <= span_ref[1])
        masks.append(jnp.where(allowed, 0.0, NEGATIVE))
    mask = jnp.concatenate([jnp.concatenate(masks, axis=1)] * GROUP, axis=0)

    scores = []
    for head in range(KH):
        at = head * columns
        queries = jnp.concatenate(
            [queries_ref[:, at + g * HD : at + (g + 1) * HD] for g in range(GROUP)], axis=0
        )
        keys = jnp.concatenate(
            [part[head * rows : (head + 1) * rows, :] for part in part_refs], axis=0
        )
        scores.append(
            lax.dot_general(
                queries, keys, (((1,), (1,)), ((), ())), preferred_element_type=jnp.float32
            )
            + mask
        )
    weights, totals = [], []
    for head in range(KH):
        top = jnp.max(scores[head], axis=1, keepdims=True)
        weight = jnp.exp2((scores[head] - top) * SCALE)
        totals.append(jnp.sum(weight, axis=1, keepdims=True))
        weights.append(weight.astype(jnp.bfloat16))
    copies = []
    for head in range(KH):
        values = jnp.concatenate(
            [part[(KH + head) * rows : (KH + head + 1) * rows, :] for part in part_refs],
            axis=0,
        )
        mixed = jnp.dot(weights[head], values, preferred_element_type=jnp.float32)
        mixed = (mixed * (1.0 / totals[head])).astype(jnp.bfloat16)
        at = head * columns
        for g in range(GROUP):
            staged[:, at + g * HD : at + (g + 1) * HD] = mixed[g * rows : (g + 1) * rows, :]
        here = pl.ds(at, columns)
        copies.append(
            pltpu.make_async_copy(staged.at[:, here], out_ref.at[:, here], sems.at[head])
        )
        copies[head].start()
    for copy in copies:
        copy.wait()


def attend(span, queries, parts):
    count = len(parts)
    rows = queries.shape[0]
    work = KH * GROUP * rows * count * rows
    return pl.pallas_call(
        partial(attend_kernel, count),
        out_shape=jax.ShapeDtypeStruct(queries.shape, jnp.bfloat16),
        in_specs=[VMEM, VMEM] + [VMEM] * count,
        out_specs=ANY,
        scratch_shapes=[
            pltpu.VMEM(queries.shape, jnp.bfloat16),
            pltpu.SemaphoreType.DMA((KH,)),
        ],
        compiler_params=pltpu.CompilerParams(vmem_limit_bytes=40 << 20),
        cost_estimate=pl.CostEstimate(
            flops=4 * work * HD, transcendentals=work, bytes_accessed=4 * work
        ),
        name="attend",
    )(span, queries, *parts)


def on_device(devices, queries, keys, values, block_order, doc_lengths):
    chips = devices // 2
    other_core = [(i, i ^ 1) for i in range(devices)]
    paired = chips & (chips - 1) == 0

    def from_chip(array, step):
        pairs = []
        for chip in range(chips):
            other = chip ^ step if paired else (chip + step) % chips
            pairs += [(2 * chip + core, 2 * other + core) for core in range(2)]
        return lax.ppermute(array, "ctx", pairs)

    def across(array):
        return lax.ppermute(array, "ctx", other_core)

    own, span = pack(block_order, doc_lengths, keys, values)
    steps = STEPS if chips == 4 else range(1, chips)
    parts = []
    for part in [own] + [from_chip(own, step) for step in steps]:
        parts += [part, across(part)]
    return attend(span, fetch(queries), parts)


STEPS = (1, 3, 2)


def solution(mesh):
    return jax.shard_map(
        partial(on_device, mesh.shape["ctx"]),
        mesh=mesh,
        in_specs=(
            P(("dp", "ctx"), None),
            P(("dp", "ctx"), None),
            P(("dp", "ctx"), None),
            P(("dp", "ctx")),
            P("dp"),
        ),
        out_specs=P(("dp", "ctx"), None),
        check_vma=False,
    )
```

```python
import math
from functools import partial

import jax
import jax.numpy as jnp
from jax import lax
from jax.experimental import pallas as pl
from jax.experimental.pallas import tpu as pltpu
from jax.sharding import PartitionSpec as P

QH = 16
KH = 4
HD = 128
BLOCK = 32
GROUP = QH // KH
TAG = 8
NEGATIVE = -1e30
SCALE = math.log2(math.e) / math.sqrt(HD)
VMEM = pl.BlockSpec(memory_space=pltpu.VMEM)
ANY = pl.BlockSpec(memory_space=pl.ANY)


def pack_kernel(
    order_ref, lengths_ref, keys_ref, values_ref, packed_ref, span_ref, order, lengths, sems
):
    rows = keys_ref.shape[0]
    copies = [
        pltpu.make_async_copy(order_ref, order, sems.at[0]),
        pltpu.make_async_copy(lengths_ref, lengths, sems.at[1]),
    ]
    for index in range(2 * KH):
        source = keys_ref if index < KH else values_ref
        copies.append(
            pltpu.make_async_copy(
                source.at[:, pl.ds(index % KH * HD, HD)],
                packed_ref.at[pl.ds(index * rows, rows), :],
                sems.at[2 + index],
            )
        )
    for copy in copies:
        copy.start()
    copies[0].wait()
    copies[1].wait()
    lane = lax.broadcasted_iota(jnp.int32, (TAG, HD), 1)
    block = jnp.where((lane // BLOCK) % 2 == 0, order[0], order[1])
    packed_ref[2 * KH * rows :, :] = block.astype(jnp.float32).astype(jnp.bfloat16)
    row = lax.broadcasted_iota(jnp.int32, (rows, 128), 0)
    position = jnp.where(row < BLOCK, order[0], order[1]) * BLOCK + row % BLOCK
    first = jnp.zeros_like(position)
    end = 0
    for doc in range(lengths.shape[0]):
        end = end + lengths[doc]
        first = jnp.where(position >= end, end, first)
    span_ref[0] = first
    span_ref[1] = position
    for copy in copies[2:]:
        copy.wait()


def pack(block_order, doc_lengths, keys, values):
    rows = keys.shape[0]
    return pl.pallas_call(
        pack_kernel,
        out_shape=(
            pltpu.VMEM((2 * KH * rows + TAG, HD), keys.dtype),
            pltpu.VMEM((2, rows, 128), jnp.int32),
        ),
        in_specs=[ANY, ANY, ANY, ANY],
        out_specs=(VMEM, VMEM),
        scratch_shapes=[
            pltpu.SMEM(block_order.shape, jnp.int32),
            pltpu.SMEM(doc_lengths.shape, jnp.int32),
            pltpu.SemaphoreType.DMA((2 + 2 * KH,)),
        ],
        name="pack",
    )(block_order, doc_lengths, keys, values)


def fetch_kernel(queries_ref, out_ref, sem):
    copy = pltpu.make_async_copy(queries_ref, out_ref, sem)
    copy.start()
    copy.wait()


def fetch(queries):
    return pl.pallas_call(
        fetch_kernel,
        out_shape=pltpu.VMEM(queries.shape, queries.dtype),
        in_specs=[ANY],
        out_specs=VMEM,
        scratch_shapes=[pltpu.SemaphoreType.DMA],
        cost_estimate=pl.CostEstimate(
            flops=0, transcendentals=0, bytes_accessed=16 * queries.size
        ),
        name="fetch",
    )(queries)


def attend_kernel(count, span_ref, queries_ref, *refs):
    part_refs = refs[:count]
    out_ref, staged, sems = refs[count:]
    rows = queries_ref.shape[0]
    columns = GROUP * HD

    lane = lax.broadcasted_iota(jnp.int32, (TAG, 128), 1)
    masks = []
    for pair in range(count // 2):
        early = part_refs[2 * pair][2 * KH * rows :, :].astype(jnp.float32)
        late = part_refs[2 * pair + 1][2 * KH * rows :, :].astype(jnp.float32)
        block = jnp.where(lane < rows, early, late).astype(jnp.int32)
        position = (block * BLOCK + lane % BLOCK)[:1, :]
        allowed = (position >= span_ref[0]) & (position <= span_ref[1])
        masks.append(jnp.where(allowed, 0.0, NEGATIVE))
    mask = jnp.concatenate([jnp.concatenate(masks, axis=1)] * GROUP, axis=0)

    scores = []
    for head in range(KH):
        at = head * columns
        queries = jnp.concatenate(
            [queries_ref[:, at + g * HD : at + (g + 1) * HD] for g in range(GROUP)], axis=0
        )
        keys = jnp.concatenate(
            [part[head * rows : (head + 1) * rows, :] for part in part_refs], axis=0
        )
        scores.append(
            lax.dot_general(
                queries, keys, (((1,), (1,)), ((), ())), preferred_element_type=jnp.float32
            )
            + mask
        )
    weights, totals = [], []
    for head in range(KH):
        top = jnp.max(scores[head], axis=1, keepdims=True)
        weight = jnp.exp2((scores[head] - top) * SCALE)
        totals.append(jnp.sum(weight, axis=1, keepdims=True))
        weights.append(weight.astype(jnp.bfloat16))
    copies = []
    for head in range(KH):
        values = jnp.concatenate(
            [part[(KH + head) * rows : (KH + head + 1) * rows, :] for part in part_refs],
            axis=0,
        )
        mixed = jnp.dot(weights[head], values, preferred_element_type=jnp.float32)
        mixed = (mixed * (1.0 / totals[head])).astype(jnp.bfloat16)
        at = head * columns
        for g in range(GROUP):
            staged[:, at + g * HD : at + (g + 1) * HD] = mixed[g * rows : (g + 1) * rows, :]
        here = pl.ds(at, columns)
        copies.append(
            pltpu.make_async_copy(staged.at[:, here], out_ref.at[:, here], sems.at[head])
        )
        copies[head].start()
    for copy in copies:
        copy.wait()


def attend(span, queries, parts):
    count = len(parts)
    rows = queries.shape[0]
    work = KH * GROUP * rows * count * rows
    return pl.pallas_call(
        partial(attend_kernel, count),
        out_shape=jax.ShapeDtypeStruct(queries.shape, jnp.bfloat16),
        in_specs=[VMEM, VMEM] + [VMEM] * count,
        out_specs=ANY,
        scratch_shapes=[
            pltpu.VMEM(queries.shape, jnp.bfloat16),
            pltpu.SemaphoreType.DMA((KH,)),
        ],
        compiler_params=pltpu.CompilerParams(vmem_limit_bytes=40 << 20),
        cost_estimate=pl.CostEstimate(
            flops=4 * work * HD, transcendentals=work, bytes_accessed=4 * work
        ),
        name="attend",
    )(span, queries, *parts)


def on_device(devices, queries, keys, values, block_order, doc_lengths):
    chips = devices // 2
    other_core = [(i, i ^ 1) for i in range(devices)]
    if chips == 4:
        routes = ROUTES
    elif chips & (chips - 1) == 0:
        routes = [[chip ^ step for chip in range(chips)] for step in range(1, chips)]
    else:
        routes = [[(chip + step) % chips for chip in range(chips)] for step in range(1, chips)]

    def along(array, route):
        pairs = [
            (2 * chip + core, 2 * route[chip] + core) for chip in range(chips) for core in range(2)
        ]
        return lax.ppermute(array, "ctx", pairs)

    def across(array):
        return lax.ppermute(array, "ctx", other_core)

    own, span = pack(block_order, doc_lengths, keys, values)
    parts = []
    for part in [own] + [along(own, route) for route in routes]:
        parts += [part, across(part)]
    return attend(span, fetch(queries), parts)


ROUTES = ((1, 0, 3, 2), (2, 3, 1, 0), (3, 2, 0, 1))


def solution(mesh):
    return jax.shard_map(
        partial(on_device, mesh.shape["ctx"]),
        mesh=mesh,
        in_specs=(
            P(("dp", "ctx"), None),
            P(("dp", "ctx"), None),
            P(("dp", "ctx"), None),
            P(("dp", "ctx")),
            P("dp"),
        ),
        out_specs=P(("dp", "ctx"), None),
        check_vma=False,
    )
```

```python
import math
from functools import partial

import jax
import jax.numpy as jnp
from jax import lax
from jax.experimental import pallas as pl
from jax.experimental.pallas import tpu as pltpu
from jax.sharding import PartitionSpec as P

QH = 16
KH = 4
HD = 128
BLOCK = 32
GROUP = QH // KH
TAG = 8
NEGATIVE = -1e30
SCALE = math.log2(math.e) / math.sqrt(HD)
VMEM = pl.BlockSpec(memory_space=pltpu.VMEM)
ANY = pl.BlockSpec(memory_space=pl.ANY)


def pack_kernel(
    order_ref, lengths_ref, keys_ref, values_ref,
    packed_ref, span_ref, order, lengths, sems,
):
    rows = keys_ref.shape[0]
    half = KH * rows
    copies = [
        pltpu.make_async_copy(order_ref, order, sems.at[0]),
        pltpu.make_async_copy(lengths_ref, lengths, sems.at[1]),
    ]
    for head in range(KH):
        for source, first in ((keys_ref, 0), (values_ref, half)):
            copies.append(
                pltpu.make_async_copy(
                    source.at[:, pl.ds(head * HD, HD)],
                    packed_ref.at[pl.ds(first + head * rows, rows), :],
                    sems.at[len(copies)],
                )
            )
    for copy in copies:
        copy.start()
    copies[0].wait()
    copies[1].wait()
    lane = lax.broadcasted_iota(jnp.int32, (TAG, HD), 1)
    block = jnp.where((lane // BLOCK) % 2 == 0, order[0], order[1])
    packed_ref[2 * half :, :] = block.astype(jnp.float32).astype(jnp.bfloat16)
    row = lax.broadcasted_iota(jnp.int32, (rows, HD), 0)
    position = jnp.where(row < BLOCK, order[0], order[1]) * BLOCK + row % BLOCK
    first = jnp.zeros_like(position)
    end = 0
    for doc in range(lengths.shape[0]):
        end = end + lengths[doc]
        first = jnp.where(position >= end, end, first)
    span_ref[0] = first
    span_ref[1] = position
    for copy in copies[2:]:
        copy.wait()


def pack(block_order, doc_lengths, keys, values):
    rows = keys.shape[0]
    half = KH * rows
    return pl.pallas_call(
        pack_kernel,
        out_shape=(
            pltpu.VMEM((2 * half + TAG, HD), keys.dtype),
            pltpu.VMEM((2, rows, HD), jnp.int32),
        ),
        in_specs=[ANY, ANY, ANY, ANY],
        out_specs=(VMEM, VMEM),
        scratch_shapes=[
            pltpu.SMEM(block_order.shape, jnp.int32),
            pltpu.SMEM(doc_lengths.shape, jnp.int32),
            pltpu.SemaphoreType.DMA((2 + 2 * KH,)),
        ],
        name="pack",
    )(block_order, doc_lengths, keys, values)


def fetch_kernel(queries_ref, out_ref, sem):
    copy = pltpu.make_async_copy(queries_ref, out_ref, sem)
    copy.start()
    copy.wait()


def fetch(queries):
    return pl.pallas_call(
        fetch_kernel,
        out_shape=pltpu.VMEM(queries.shape, queries.dtype),
        in_specs=[ANY],
        out_specs=VMEM,
        scratch_shapes=[pltpu.SemaphoreType.DMA],
        cost_estimate=pl.CostEstimate(
            flops=0, transcendentals=0, bytes_accessed=16 * queries.size
        ),
        name="fetch",
    )(queries)


def attend_kernel(count, first, last, span_ref, queries_ref, *refs):
    rows = queries_ref.shape[0]
    half = KH * rows
    columns = GROUP * HD
    part_refs, refs = refs[:count], refs[count:]
    if not first:
        (top_in, total_in, mixed_in), refs = refs[:3], refs[3:]
    if last:
        out_ref, staged, sems = refs
    else:
        top_out, total_out, mixed_out = refs

    lane = lax.broadcasted_iota(jnp.int32, (TAG, HD), 1)
    masks = []
    for early, late in zip(part_refs[::2], part_refs[1::2]):
        block = jnp.where(
            lane < rows,
            early[2 * half :, :].astype(jnp.float32),
            late[2 * half :, :].astype(jnp.float32),
        ).astype(jnp.int32)
        position = (block * BLOCK + lane % BLOCK)[:1, :]
        allowed = (position >= span_ref[0]) & (position <= span_ref[1])
        masks.append(jnp.where(allowed, 0.0, NEGATIVE))
    mask = jnp.concatenate([jnp.concatenate(masks, axis=1)] * GROUP, axis=0)

    scores = []
    for head in range(KH):
        at = head * columns
        queries = jnp.concatenate(
            [queries_ref[:, at + g * HD : at + (g + 1) * HD] for g in range(GROUP)], axis=0
        )
        keys = jnp.concatenate(
            [part[head * rows : (head + 1) * rows, :] for part in part_refs], axis=0
        )
        scores.append(
            lax.dot_general(
                queries, keys, (((1,), (1,)), ((), ())), preferred_element_type=jnp.float32
            )
            + mask
        )
    tops, weights, totals = [], [], []
    for head in range(KH):
        top = jnp.max(scores[head], axis=1, keepdims=True)
        if not first:
            top = jnp.maximum(top, top_in[head])
            wide = jnp.concatenate([top] * len(masks), axis=1)
            weight = jnp.exp2((scores[head] - wide) * SCALE)
        else:
            weight = jnp.exp2((scores[head] - top) * SCALE)
        tops.append(top)
        totals.append(jnp.sum(weight, axis=1, keepdims=True))
        weights.append(weight.astype(jnp.bfloat16))
    copies = []
    for head in range(KH):
        values = jnp.concatenate(
            [part[half + head * rows : half + (head + 1) * rows, :] for part in part_refs],
            axis=0,
        )
        mixed = jnp.dot(weights[head], values, preferred_element_type=jnp.float32)
        total = totals[head]
        if not first:
            factor = jnp.exp2((top_in[head] - tops[head]) * SCALE)
            total = total + total_in[head] * factor
            mixed = mixed + mixed_in[head] * factor
        if not last:
            top_out[head] = jnp.broadcast_to(tops[head], (GROUP * rows, HD))
            total_out[head] = jnp.broadcast_to(total, (GROUP * rows, HD))
            mixed_out[head] = mixed
            continue
        mixed = (mixed * (1.0 / total)).astype(jnp.bfloat16)
        at = head * columns
        for g in range(GROUP):
            staged[:, at + g * HD : at + (g + 1) * HD] = mixed[g * rows : (g + 1) * rows, :]
        here = pl.ds(at, columns)
        copies.append(
            pltpu.make_async_copy(staged.at[:, here], out_ref.at[:, here], sems.at[head])
        )
        copies[head].start()
    for copy in copies:
        copy.wait()


def attend(span, queries, parts, state, last):
    rows = queries.shape[0]
    work = KH * GROUP * rows * len(parts) * rows
    out_shape = (pltpu.VMEM((KH, GROUP * rows, HD), jnp.float32),) * 3
    scratch = []
    if last:
        out_shape = jax.ShapeDtypeStruct(queries.shape, jnp.bfloat16)
        scratch = [pltpu.VMEM(queries.shape, jnp.bfloat16), pltpu.SemaphoreType.DMA((KH,))]
    return pl.pallas_call(
        partial(attend_kernel, len(parts), not state, last),
        out_shape=out_shape,
        in_specs=[VMEM] * (2 + len(parts) + len(state)),
        out_specs=ANY if last else (VMEM, VMEM, VMEM),
        scratch_shapes=scratch,
        compiler_params=pltpu.CompilerParams(vmem_limit_bytes=40 << 20),
        cost_estimate=pl.CostEstimate(
            flops=4 * work * HD, transcendentals=work, bytes_accessed=4 * work
        ),
        name="finish" if last else "begin",
    )(span, queries, *parts, *state)


def on_device(devices, queries, keys, values, block_order, doc_lengths):
    chips = devices // 2
    other_core = [(i, i ^ 1) for i in range(devices)]
    if chips == 4:
        routes = ROUTES
    elif chips & (chips - 1) == 0:
        routes = [[chip ^ step for chip in range(chips)] for step in range(1, chips)]
    else:
        routes = [[(chip + step) % chips for chip in range(chips)] for step in range(1, chips)]

    def along(array, route):
        pairs = [
            (2 * chip + core, 2 * route[chip] + core) for chip in range(chips) for core in range(2)
        ]
        return lax.ppermute(array, "ctx", pairs)

    def across(array):
        return lax.ppermute(array, "ctx", other_core)

    own, span = pack(block_order, doc_lengths, keys, values)
    rows = fetch(queries)
    early = [own, across(own)]
    late = []
    for index, route in enumerate(reversed(routes)):
        part = along(own, route)
        if index == 0:
            rows, part = lax.optimization_barrier((rows, part))
        early.append(part)
        late.append(across(part))
    state = attend(span, rows, early + late[: len(late) % 2], (), False)
    return attend(span, rows, late[len(late) % 2 :], state, True)


ROUTES = ((1, 0, 3, 2), (2, 3, 1, 0), (3, 2, 0, 1))


def solution(mesh):
    return jax.shard_map(
        partial(on_device, mesh.shape["ctx"]),
        mesh=mesh,
        in_specs=(
            P(("dp", "ctx"), None),
            P(("dp", "ctx"), None),
            P(("dp", "ctx"), None),
            P(("dp", "ctx")),
            P("dp"),
        ),
        out_specs=P(("dp", "ctx"), None),
        check_vma=False,
    )
```

```python
import math
from functools import partial

import jax
import jax.numpy as jnp
from jax import lax
from jax.experimental import pallas as pl
from jax.experimental.pallas import tpu as pltpu
from jax.sharding import PartitionSpec as P

QH = 16
KH = 4
HD = 128
BLOCK = 32
GROUP = QH // KH
TAG = 8
NEGATIVE = -1e30
SCALE = math.log2(math.e) / math.sqrt(HD)
VMEM = pl.BlockSpec(memory_space=pltpu.VMEM)
ANY = pl.BlockSpec(memory_space=pl.ANY)


def pack_kernel(
    order_ref, lengths_ref, keys_ref, values_ref,
    packed_ref, span_ref, order, lengths, sems,
):
    rows = keys_ref.shape[0]
    half = KH * rows
    copies = [
        pltpu.make_async_copy(order_ref, order, sems.at[0]),
        pltpu.make_async_copy(lengths_ref, lengths, sems.at[1]),
    ]
    for head in range(KH):
        for source, first in ((keys_ref, 0), (values_ref, half)):
            copies.append(
                pltpu.make_async_copy(
                    source.at[:, pl.ds(head * HD, HD)],
                    packed_ref.at[pl.ds(first + head * rows, rows), :],
                    sems.at[len(copies)],
                )
            )
    for copy in copies:
        copy.start()
    copies[0].wait()
    copies[1].wait()
    lane = lax.broadcasted_iota(jnp.int32, (TAG, HD), 1)
    block = jnp.where((lane // BLOCK) % 2 == 0, order[0], order[1])
    packed_ref[2 * half :, :] = block.astype(jnp.float32).astype(jnp.bfloat16)
    row = lax.broadcasted_iota(jnp.int32, (rows, HD), 0)
    position = jnp.where(row < BLOCK, order[0], order[1]) * BLOCK + row % BLOCK
    first = jnp.zeros_like(position)
    end = 0
    for doc in range(lengths.shape[0]):
        end = end + lengths[doc]
        first = jnp.where(position >= end, end, first)
    span_ref[0] = first
    span_ref[1] = position
    for copy in copies[2:]:
        copy.wait()


def pack(block_order, doc_lengths, keys, values):
    rows = keys.shape[0]
    half = KH * rows
    return pl.pallas_call(
        pack_kernel,
        out_shape=(
            pltpu.VMEM((2 * half + TAG, HD), keys.dtype),
            pltpu.VMEM((2, rows, HD), jnp.int32),
        ),
        in_specs=[ANY, ANY, ANY, ANY],
        out_specs=(VMEM, VMEM),
        scratch_shapes=[
            pltpu.SMEM(block_order.shape, jnp.int32),
            pltpu.SMEM(doc_lengths.shape, jnp.int32),
            pltpu.SemaphoreType.DMA((2 + 2 * KH,)),
        ],
        name="pack",
    )(block_order, doc_lengths, keys, values)


def fetch_kernel(queries_ref, out_ref, sem):
    copy = pltpu.make_async_copy(queries_ref, out_ref, sem)
    copy.start()
    copy.wait()


def fetch(queries):
    return pl.pallas_call(
        fetch_kernel,
        out_shape=pltpu.VMEM(queries.shape, queries.dtype),
        in_specs=[ANY],
        out_specs=VMEM,
        scratch_shapes=[pltpu.SemaphoreType.DMA],
        cost_estimate=pl.CostEstimate(
            flops=0, transcendentals=0, bytes_accessed=16 * queries.size
        ),
        name="fetch",
    )(queries)


def attend_kernel(count, first, last, span_ref, queries_ref, *refs):
    rows = queries_ref.shape[0]
    half = KH * rows
    columns = GROUP * HD
    part_refs, refs = refs[:count], refs[count:]
    if not first:
        (top_in, total_in, mixed_in), refs = refs[:3], refs[3:]
    if last:
        out_ref, staged, sems = refs
    else:
        top_out, total_out, mixed_out = refs

    lane = lax.broadcasted_iota(jnp.int32, (TAG, HD), 1)
    masks = []
    for early, late in zip(part_refs[::2], part_refs[1::2]):
        block = jnp.where(
            lane < rows,
            early[2 * half :, :].astype(jnp.float32),
            late[2 * half :, :].astype(jnp.float32),
        ).astype(jnp.int32)
        position = (block * BLOCK + lane % BLOCK)[:1, :]
        allowed = (position >= span_ref[0]) & (position <= span_ref[1])
        masks.append(jnp.where(allowed, 0.0, NEGATIVE))
    mask = jnp.concatenate([jnp.concatenate(masks, axis=1)] * GROUP, axis=0)

    scores = []
    for head in range(KH):
        at = head * columns
        queries = jnp.concatenate(
            [queries_ref[:, at + g * HD : at + (g + 1) * HD] for g in range(GROUP)], axis=0
        )
        keys = jnp.concatenate(
            [part[head * rows : (head + 1) * rows, :] for part in part_refs], axis=0
        )
        scores.append(
            lax.dot_general(
                queries, keys, (((1,), (1,)), ((), ())), preferred_element_type=jnp.float32
            )
            + mask
        )
    tops, weights, totals = [], [], []
    for head in range(KH):
        top = jnp.max(scores[head], axis=1, keepdims=True)
        if not first:
            top = jnp.maximum(top, top_in[head])
            wide = jnp.concatenate([top] * len(masks), axis=1)
            weight = jnp.exp2((scores[head] - wide) * SCALE)
        else:
            weight = jnp.exp2((scores[head] - top) * SCALE)
        tops.append(top)
        totals.append(jnp.sum(weight, axis=1, keepdims=True))
        weights.append(weight.astype(jnp.bfloat16))
    copies = []
    for head in range(KH):
        values = jnp.concatenate(
            [part[half + head * rows : half + (head + 1) * rows, :] for part in part_refs],
            axis=0,
        )
        mixed = jnp.dot(weights[head], values, preferred_element_type=jnp.float32)
        total = totals[head]
        if not first:
            factor = jnp.exp2((top_in[head] - tops[head]) * SCALE)
            total = total + total_in[head] * factor
            mixed = mixed + mixed_in[head] * factor
        if not last:
            top_out[head] = jnp.broadcast_to(tops[head], (GROUP * rows, HD))
            total_out[head] = jnp.broadcast_to(total, (GROUP * rows, HD))
            mixed_out[head] = mixed
            continue
        mixed = (mixed * (1.0 / total)).astype(jnp.bfloat16)
        at = head * columns
        for g in range(GROUP):
            staged[:, at + g * HD : at + (g + 1) * HD] = mixed[g * rows : (g + 1) * rows, :]
        here = pl.ds(at, columns)
        copies.append(
            pltpu.make_async_copy(staged.at[:, here], out_ref.at[:, here], sems.at[head])
        )
        copies[head].start()
    for copy in copies:
        copy.wait()


def attend(span, queries, parts, state, last):
    rows = queries.shape[0]
    work = KH * GROUP * rows * len(parts) * rows
    out_shape = (pltpu.VMEM((KH, GROUP * rows, HD), jnp.float32),) * 3
    scratch = []
    if last:
        out_shape = jax.ShapeDtypeStruct(queries.shape, jnp.bfloat16)
        scratch = [pltpu.VMEM(queries.shape, jnp.bfloat16), pltpu.SemaphoreType.DMA((KH,))]
    return pl.pallas_call(
        partial(attend_kernel, len(parts), not state, last),
        out_shape=out_shape,
        in_specs=[VMEM] * (2 + len(parts) + len(state)),
        out_specs=ANY if last else (VMEM, VMEM, VMEM),
        scratch_shapes=scratch,
        compiler_params=pltpu.CompilerParams(vmem_limit_bytes=40 << 20),
        cost_estimate=pl.CostEstimate(
            flops=4 * work * HD, transcendentals=work, bytes_accessed=4 * work
        ),
        name="finish" if last else "begin",
    )(span, queries, *parts, *state)


def on_device(devices, queries, keys, values, block_order, doc_lengths):
    chips = devices // 2
    other_core = [(i, i ^ 1) for i in range(devices)]
    if chips == 4:
        routes = ROUTES
    elif chips & (chips - 1) == 0:
        routes = [[[chip ^ step for chip in range(chips)]] * 2 for step in range(1, chips)]
    else:
        routes = [
            [[(chip + step) % chips for chip in range(chips)]] * 2 for step in range(1, chips)
        ]

    def along(array, route):
        pairs = [
            (2 * chip + core, 2 * route[core][chip] + core)
            for chip in range(chips)
            for core in range(2)
        ]
        return lax.ppermute(array, "ctx", pairs)

    def across(array):
        return lax.ppermute(array, "ctx", other_core)

    own, span = pack(block_order, doc_lengths, keys, values)
    rows = fetch(queries)
    early = [own, across(own)]
    late = []
    for index, route in enumerate(routes):
        part = along(own, route)
        if index == 0:
            rows, part = lax.optimization_barrier((rows, part))
        early.append(part)
        late.append(across(part))
    state = attend(span, rows, early + late[: len(late) % 2], (), False)
    return attend(span, rows, late[len(late) % 2 :], state, True)


ROUTES = (((1, 2, 3, 0), (3, 2, 0, 1)), ((2, 3, 0, 1), (2, 3, 1, 0)), ((3, 0, 1, 2), (1, 0, 3, 2)))


def solution(mesh):
    return jax.shard_map(
        partial(on_device, mesh.shape["ctx"]),
        mesh=mesh,
        in_specs=(
            P(("dp", "ctx"), None),
            P(("dp", "ctx"), None),
            P(("dp", "ctx"), None),
            P(("dp", "ctx")),
            P("dp"),
        ),
        out_specs=P(("dp", "ctx"), None),
        check_vma=False,
    )
```

```python
import math
from functools import partial

import jax
import jax.numpy as jnp
from jax import lax
from jax.experimental import pallas as pl
from jax.experimental.pallas import tpu as pltpu
from jax.sharding import PartitionSpec as P

QH = 16
KH = 4
HD = 128
BLOCK = 32
GROUP = QH // KH
TAG = 8
NEGATIVE = -1e30
SCALE = math.log2(math.e) / math.sqrt(HD)
VMEM = pl.BlockSpec(memory_space=pltpu.VMEM)
ANY = pl.BlockSpec(memory_space=pl.ANY)


def pack_kernel(
    order_ref, lengths_ref, keys_ref, values_ref,
    packed_ref, span_ref, order, lengths, sems,
):
    rows = keys_ref.shape[0]
    half = KH * rows
    copies = [
        pltpu.make_async_copy(order_ref, order, sems.at[0]),
        pltpu.make_async_copy(lengths_ref, lengths, sems.at[1]),
    ]
    for head in range(KH):
        for source, first in ((keys_ref, 0), (values_ref, half)):
            copies.append(
                pltpu.make_async_copy(
                    source.at[:, pl.ds(head * HD, HD)],
                    packed_ref.at[pl.ds(first + head * rows, rows), :],
                    sems.at[len(copies)],
                )
            )
    for copy in copies:
        copy.start()
    copies[0].wait()
    copies[1].wait()
    lane = lax.broadcasted_iota(jnp.int32, (TAG, HD), 1)
    block = jnp.where((lane // BLOCK) % 2 == 0, order[0], order[1])
    packed_ref[2 * half :, :] = block.astype(jnp.float32).astype(jnp.bfloat16)
    row = lax.broadcasted_iota(jnp.int32, (rows, HD), 0)
    position = jnp.where(row < BLOCK, order[0], order[1]) * BLOCK + row % BLOCK
    first = jnp.zeros_like(position)
    end = 0
    for doc in range(lengths.shape[0]):
        end = end + lengths[doc]
        first = jnp.where(position >= end, end, first)
    span_ref[0] = first
    span_ref[1] = position
    for copy in copies[2:]:
        copy.wait()


def pack(block_order, doc_lengths, keys, values):
    rows = keys.shape[0]
    half = KH * rows
    return pl.pallas_call(
        pack_kernel,
        out_shape=(
            pltpu.VMEM((2 * half + TAG, HD), keys.dtype),
            pltpu.VMEM((2, rows, HD), jnp.int32),
        ),
        in_specs=[ANY, ANY, ANY, ANY],
        out_specs=(VMEM, VMEM),
        scratch_shapes=[
            pltpu.SMEM(block_order.shape, jnp.int32),
            pltpu.SMEM(doc_lengths.shape, jnp.int32),
            pltpu.SemaphoreType.DMA((2 + 2 * KH,)),
        ],
        name="pack",
    )(block_order, doc_lengths, keys, values)


def fetch_kernel(queries_ref, out_ref, sem):
    copy = pltpu.make_async_copy(queries_ref, out_ref, sem)
    copy.start()
    copy.wait()


def fetch(queries):
    return pl.pallas_call(
        fetch_kernel,
        out_shape=pltpu.VMEM(queries.shape, queries.dtype),
        in_specs=[ANY],
        out_specs=VMEM,
        scratch_shapes=[pltpu.SemaphoreType.DMA],
        cost_estimate=pl.CostEstimate(
            flops=0, transcendentals=0, bytes_accessed=16 * queries.size
        ),
        name="fetch",
    )(queries)


def attend_kernel(count, first, last, span_ref, queries_ref, *refs):
    rows = queries_ref.shape[0]
    half = KH * rows
    columns = GROUP * HD
    part_refs, refs = refs[:count], refs[count:]
    if not first:
        (top_in, total_in, mixed_in), refs = refs[:3], refs[3:]
    if last:
        out_ref, staged, sems = refs
    else:
        top_out, total_out, mixed_out = refs

    lane = lax.broadcasted_iota(jnp.int32, (TAG, HD), 1)
    masks = []
    for early, late in zip(part_refs[::2], part_refs[1::2]):
        block = jnp.where(
            lane < rows,
            early[2 * half :, :].astype(jnp.float32),
            late[2 * half :, :].astype(jnp.float32),
        ).astype(jnp.int32)
        position = (block * BLOCK + lane % BLOCK)[:1, :]
        allowed = (position >= span_ref[0]) & (position <= span_ref[1])
        masks.append(jnp.where(allowed, 0.0, NEGATIVE))
    mask = jnp.concatenate([jnp.concatenate(masks, axis=1)] * GROUP, axis=0)

    scores = []
    for head in range(KH):
        at = head * columns
        queries = jnp.concatenate(
            [queries_ref[:, at + g * HD : at + (g + 1) * HD] for g in range(GROUP)], axis=0
        )
        keys = jnp.concatenate(
            [part[head * rows : (head + 1) * rows, :] for part in part_refs], axis=0
        )
        scores.append(
            lax.dot_general(
                queries, keys, (((1,), (1,)), ((), ())), preferred_element_type=jnp.float32
            )
            + mask
        )
    tops, weights, totals = [], [], []
    for head in range(KH):
        top = jnp.max(scores[head], axis=1, keepdims=True)
        if not first:
            top = jnp.maximum(top, top_in[head])
            wide = jnp.concatenate([top] * len(masks), axis=1)
            weight = jnp.exp2((scores[head] - wide) * SCALE)
        else:
            weight = jnp.exp2((scores[head] - top) * SCALE)
        tops.append(top)
        totals.append(jnp.sum(weight, axis=1, keepdims=True))
        weights.append(weight.astype(jnp.bfloat16))
    copies = []
    for head in range(KH):
        values = jnp.concatenate(
            [part[half + head * rows : half + (head + 1) * rows, :] for part in part_refs],
            axis=0,
        )
        mixed = jnp.dot(weights[head], values, preferred_element_type=jnp.float32)
        total = totals[head]
        if not first:
            factor = jnp.exp2((top_in[head] - tops[head]) * SCALE)
            total = total + total_in[head] * factor
            mixed = mixed + mixed_in[head] * factor
        if not last:
            top_out[head] = jnp.broadcast_to(tops[head], (GROUP * rows, HD))
            total_out[head] = jnp.broadcast_to(total, (GROUP * rows, HD))
            mixed_out[head] = mixed
            continue
        mixed = (mixed * (1.0 / total)).astype(jnp.bfloat16)
        at = head * columns
        for g in range(GROUP):
            staged[:, at + g * HD : at + (g + 1) * HD] = mixed[g * rows : (g + 1) * rows, :]
        here = pl.ds(at, columns)
        copies.append(
            pltpu.make_async_copy(staged.at[:, here], out_ref.at[:, here], sems.at[head])
        )
        copies[head].start()
    for copy in copies:
        copy.wait()


def attend(span, queries, parts, state, last):
    rows = queries.shape[0]
    work = KH * GROUP * rows * len(parts) * rows
    out_shape = (pltpu.VMEM((KH, GROUP * rows, HD), jnp.float32),) * 3
    scratch = []
    if last:
        out_shape = jax.ShapeDtypeStruct(queries.shape, jnp.bfloat16)
        scratch = [pltpu.VMEM(queries.shape, jnp.bfloat16), pltpu.SemaphoreType.DMA((KH,))]
    return pl.pallas_call(
        partial(attend_kernel, len(parts), not state, last),
        out_shape=out_shape,
        in_specs=[VMEM] * (2 + len(parts) + len(state)),
        out_specs=ANY if last else (VMEM, VMEM, VMEM),
        scratch_shapes=scratch,
        compiler_params=pltpu.CompilerParams(vmem_limit_bytes=40 << 20),
        cost_estimate=pl.CostEstimate(
            flops=4 * work * HD, transcendentals=work, bytes_accessed=4 * work
        ),
        name="finish" if last else "begin",
    )(span, queries, *parts, *state)


def on_device(devices, queries, keys, values, block_order, doc_lengths):
    chips = devices // 2
    other_core = [(i, i ^ 1) for i in range(devices)]
    if chips == 4:
        routes = ROUTES
    elif chips & (chips - 1) == 0:
        routes = [[[chip ^ step for chip in range(chips)]] * 2 for step in range(1, chips)]
    else:
        routes = [
            [[(chip + step) % chips for chip in range(chips)]] * 2 for step in range(1, chips)
        ]

    def along(array, route):
        pairs = [
            (2 * chip + core, 2 * route[core][chip] + core)
            for chip in range(chips)
            for core in range(2)
        ]
        return lax.ppermute(array, "ctx", pairs)

    def across(array):
        return lax.ppermute(array, "ctx", other_core)

    own, span = pack(block_order, doc_lengths, keys, values)
    rows = fetch(queries)
    early = [own, across(own)]
    late = []
    for index, route in enumerate(routes):
        part = along(own, route)
        if index == 0:
            rows, part = lax.optimization_barrier((rows, part))
        early.append(part)
        late.append(across(part))
    state = attend(span, rows, early + late[: len(late) % 2], (), False)
    return attend(span, rows, late[len(late) % 2 :], state, True)


ROUTES = (((2, 0, 3, 1), (3, 2, 0, 1)), ((1, 3, 0, 2), (2, 3, 1, 0)), ((3, 2, 1, 0), (1, 0, 3, 2)))


def solution(mesh):
    return jax.shard_map(
        partial(on_device, mesh.shape["ctx"]),
        mesh=mesh,
        in_specs=(
            P(("dp", "ctx"), None),
            P(("dp", "ctx"), None),
            P(("dp", "ctx"), None),
            P(("dp", "ctx")),
            P("dp"),
        ),
        out_specs=P(("dp", "ctx"), None),
        check_vma=False,
    )
```

```python
import math
from functools import partial

import jax
import jax.numpy as jnp
from jax import lax
from jax.experimental import pallas as pl
from jax.experimental.pallas import tpu as pltpu
from jax.sharding import PartitionSpec as P

QH = 16
KH = 4
HD = 128
BLOCK = 32
GROUP = QH // KH
TAG = 8
NEGATIVE = -1e30
SCALE = math.log2(math.e) / math.sqrt(HD)
VMEM = pl.BlockSpec(memory_space=pltpu.VMEM)
ANY = pl.BlockSpec(memory_space=pl.ANY)


def pack_kernel(
    order_ref, lengths_ref, keys_ref, values_ref,
    packed_ref, span_ref, order, lengths, sems,
):
    rows = keys_ref.shape[0]
    half = KH * rows
    copies = [
        pltpu.make_async_copy(order_ref, order, sems.at[0]),
        pltpu.make_async_copy(lengths_ref, lengths, sems.at[1]),
    ]
    for head in range(KH):
        for source, first in ((keys_ref, 0), (values_ref, half)):
            copies.append(
                pltpu.make_async_copy(
                    source.at[:, pl.ds(head * HD, HD)],
                    packed_ref.at[pl.ds(first + head * rows, rows), :],
                    sems.at[len(copies)],
                )
            )
    for copy in copies:
        copy.start()
    copies[0].wait()
    copies[1].wait()
    lane = lax.broadcasted_iota(jnp.int32, (TAG, HD), 1)
    block = jnp.where((lane // BLOCK) % 2 == 0, order[0], order[1])
    packed_ref[2 * half :, :] = block.astype(jnp.float32).astype(jnp.bfloat16)
    row = lax.broadcasted_iota(jnp.int32, (rows, HD), 0)
    position = jnp.where(row < BLOCK, order[0], order[1]) * BLOCK + row % BLOCK
    first = jnp.zeros_like(position)
    end = 0
    for doc in range(lengths.shape[0]):
        end = end + lengths[doc]
        first = jnp.where(position >= end, end, first)
    span_ref[0] = first
    span_ref[1] = position
    for copy in copies[2:]:
        copy.wait()


def pack(block_order, doc_lengths, keys, values):
    rows = keys.shape[0]
    half = KH * rows
    return pl.pallas_call(
        pack_kernel,
        out_shape=(
            pltpu.VMEM((2 * half + TAG, HD), keys.dtype),
            pltpu.VMEM((2, rows, HD), jnp.int32),
        ),
        in_specs=[ANY, ANY, ANY, ANY],
        out_specs=(VMEM, VMEM),
        scratch_shapes=[
            pltpu.SMEM(block_order.shape, jnp.int32),
            pltpu.SMEM(doc_lengths.shape, jnp.int32),
            pltpu.SemaphoreType.DMA((2 + 2 * KH,)),
        ],
        name="pack",
    )(block_order, doc_lengths, keys, values)


def fetch_kernel(queries_ref, out_ref, sem):
    copy = pltpu.make_async_copy(queries_ref, out_ref, sem)
    copy.start()
    copy.wait()


def fetch(queries):
    return pl.pallas_call(
        fetch_kernel,
        out_shape=pltpu.VMEM(queries.shape, queries.dtype),
        in_specs=[ANY],
        out_specs=VMEM,
        scratch_shapes=[pltpu.SemaphoreType.DMA],
        cost_estimate=pl.CostEstimate(
            flops=0, transcendentals=0, bytes_accessed=16 * queries.size
        ),
        name="fetch",
    )(queries)


def attend_kernel(count, first, last, span_ref, queries_ref, *refs):
    rows = queries_ref.shape[0]
    half = KH * rows
    columns = GROUP * HD
    part_refs, refs = refs[:count], refs[count:]
    if not first:
        (top_in, total_in, mixed_in), refs = refs[:3], refs[3:]
    if last:
        out_ref, staged, sems = refs
    else:
        top_out, total_out, mixed_out = refs

    lane = lax.broadcasted_iota(jnp.int32, (TAG, HD), 1)
    masks = []
    for early, late in zip(part_refs[::2], part_refs[1::2]):
        block = jnp.where(
            lane < rows,
            early[2 * half :, :].astype(jnp.float32),
            late[2 * half :, :].astype(jnp.float32),
        ).astype(jnp.int32)
        position = (block * BLOCK + lane % BLOCK)[:1, :]
        allowed = (position >= span_ref[0]) & (position <= span_ref[1])
        masks.append(jnp.where(allowed, 0.0, NEGATIVE))
    mask = jnp.concatenate([jnp.concatenate(masks, axis=1)] * GROUP, axis=0)

    scores = []
    for head in range(KH):
        at = head * columns
        queries = jnp.concatenate(
            [queries_ref[:, at + g * HD : at + (g + 1) * HD] for g in range(GROUP)], axis=0
        )
        keys = jnp.concatenate(
            [part[head * rows : (head + 1) * rows, :] for part in part_refs], axis=0
        )
        scores.append(
            lax.dot_general(
                queries, keys, (((1,), (1,)), ((), ())), preferred_element_type=jnp.float32
            )
            + mask
        )
    tops, weights, totals = [], [], []
    for head in range(KH):
        top = jnp.max(scores[head], axis=1, keepdims=True)
        if not first:
            top = jnp.maximum(top, top_in[head])
            wide = jnp.concatenate([top] * len(masks), axis=1)
            weight = jnp.exp2((scores[head] - wide) * SCALE)
        else:
            weight = jnp.exp2((scores[head] - top) * SCALE)
        tops.append(top)
        totals.append(jnp.sum(weight, axis=1, keepdims=True))
        weights.append(weight.astype(jnp.bfloat16))
    copies = []
    for head in range(KH):
        values = jnp.concatenate(
            [part[half + head * rows : half + (head + 1) * rows, :] for part in part_refs],
            axis=0,
        )
        mixed = jnp.dot(weights[head], values, preferred_element_type=jnp.float32)
        total = totals[head]
        if not first:
            factor = jnp.exp2((top_in[head] - tops[head]) * SCALE)
            total = total + total_in[head] * factor
            mixed = mixed + mixed_in[head] * factor
        if not last:
            top_out[head] = jnp.broadcast_to(tops[head], (GROUP * rows, HD))
            total_out[head] = jnp.broadcast_to(total, (GROUP * rows, HD))
            mixed_out[head] = mixed
            continue
        mixed = (mixed * (1.0 / total)).astype(jnp.bfloat16)
        at = head * columns
        for g in range(GROUP):
            staged[:, at + g * HD : at + (g + 1) * HD] = mixed[g * rows : (g + 1) * rows, :]
        here = pl.ds(at, columns)
        copies.append(
            pltpu.make_async_copy(staged.at[:, here], out_ref.at[:, here], sems.at[head])
        )
        copies[head].start()
    for copy in copies:
        copy.wait()


def attend(span, queries, parts, state, last):
    rows = queries.shape[0]
    work = KH * GROUP * rows * len(parts) * rows
    out_shape = (pltpu.VMEM((KH, GROUP * rows, HD), jnp.float32),) * 3
    scratch = []
    if last:
        out_shape = jax.ShapeDtypeStruct(queries.shape, jnp.bfloat16)
        scratch = [pltpu.VMEM(queries.shape, jnp.bfloat16), pltpu.SemaphoreType.DMA((KH,))]
    return pl.pallas_call(
        partial(attend_kernel, len(parts), not state, last),
        out_shape=out_shape,
        in_specs=[VMEM] * (2 + len(parts) + len(state)),
        out_specs=ANY if last else (VMEM, VMEM, VMEM),
        scratch_shapes=scratch,
        compiler_params=pltpu.CompilerParams(vmem_limit_bytes=40 << 20),
        cost_estimate=pl.CostEstimate(
            flops=4 * work * HD, transcendentals=work, bytes_accessed=4 * work
        ),
        name="finish" if last else "begin",
    )(span, queries, *parts, *state)


def on_device(devices, queries, keys, values, block_order, doc_lengths):
    chips = devices // 2
    other_core = [(i, i ^ 1) for i in range(devices)]
    if chips == 4:
        routes = ROUTES
    elif chips & (chips - 1) == 0:
        routes = [[[chip ^ step for chip in range(chips)]] * 2 for step in range(1, chips)]
    else:
        routes = [
            [[(chip + step) % chips for chip in range(chips)]] * 2 for step in range(1, chips)
        ]

    def along(array, route):
        pairs = [
            (2 * chip + core, 2 * route[core][chip] + core)
            for chip in range(chips)
            for core in range(2)
        ]
        return lax.ppermute(array, "ctx", pairs)

    def across(array):
        return lax.ppermute(array, "ctx", other_core)

    own, span = pack(block_order, doc_lengths, keys, values)
    rows = fetch(queries)
    early = [own, across(own)]
    late = []
    for index, route in enumerate(routes):
        part = along(own, route)
        if index == 0:
            rows, part = lax.optimization_barrier((rows, part))
        early.append(part)
        late.append(across(part))
    state = attend(span, rows, early + late[: len(late) % 2], (), False)
    return attend(span, rows, late[len(late) % 2 :], state, True)


ROUTES = (((2, 3, 0, 1), (3, 2, 0, 1)), ((1, 0, 3, 2), (1, 0, 3, 2)), ((3, 2, 1, 0), (2, 3, 1, 0)))


def solution(mesh):
    return jax.shard_map(
        partial(on_device, mesh.shape["ctx"]),
        mesh=mesh,
        in_specs=(
            P(("dp", "ctx"), None),
            P(("dp", "ctx"), None),
            P(("dp", "ctx"), None),
            P(("dp", "ctx")),
            P("dp"),
        ),
        out_specs=P(("dp", "ctx"), None),
        check_vma=False,
    )
```

```python
import math
from functools import partial

import jax
import jax.numpy as jnp
from jax import lax
from jax.experimental import pallas as pl
from jax.experimental.pallas import tpu as pltpu
from jax.sharding import PartitionSpec as P

QH = 16
KH = 4
HD = 128
BLOCK = 32
GROUP = QH // KH
TAG = 8
NEGATIVE = -1e30
SCALE = math.log2(math.e) / math.sqrt(HD)
VMEM = pl.BlockSpec(memory_space=pltpu.VMEM)
ANY = pl.BlockSpec(memory_space=pl.ANY)


def pack_kernel(
    order_ref, lengths_ref, keys_ref, values_ref,
    packed_ref, span_ref, order, lengths, sems,
):
    rows = keys_ref.shape[0]
    half = KH * rows
    copies = [
        pltpu.make_async_copy(order_ref, order, sems.at[0]),
        pltpu.make_async_copy(lengths_ref, lengths, sems.at[1]),
    ]
    for head in range(KH):
        for source, first in ((keys_ref, 0), (values_ref, half)):
            copies.append(
                pltpu.make_async_copy(
                    source.at[:, pl.ds(head * HD, HD)],
                    packed_ref.at[pl.ds(first + head * rows, rows), :],
                    sems.at[len(copies)],
                )
            )
    for copy in copies:
        copy.start()
    copies[0].wait()
    copies[1].wait()
    lane = lax.broadcasted_iota(jnp.int32, (TAG, HD), 1)
    block = jnp.where((lane // BLOCK) % 2 == 0, order[0], order[1])
    packed_ref[2 * half :, :] = block.astype(jnp.float32).astype(jnp.bfloat16)
    row = lax.broadcasted_iota(jnp.int32, (rows, HD), 0)
    position = jnp.where(row < BLOCK, order[0], order[1]) * BLOCK + row % BLOCK
    first = jnp.zeros_like(position)
    end = 0
    for doc in range(lengths.shape[0]):
        end = end + lengths[doc]
        first = jnp.where(position >= end, end, first)
    span_ref[0] = first
    span_ref[1] = position
    for copy in copies[2:]:
        copy.wait()


def pack(block_order, doc_lengths, keys, values):
    rows = keys.shape[0]
    half = KH * rows
    return pl.pallas_call(
        pack_kernel,
        out_shape=(
            pltpu.VMEM((2 * half + TAG, HD), keys.dtype),
            pltpu.VMEM((2, rows, HD), jnp.int32),
        ),
        in_specs=[ANY, ANY, ANY, ANY],
        out_specs=(VMEM, VMEM),
        scratch_shapes=[
            pltpu.SMEM(block_order.shape, jnp.int32),
            pltpu.SMEM(doc_lengths.shape, jnp.int32),
            pltpu.SemaphoreType.DMA((2 + 2 * KH,)),
        ],
        name="pack",
    )(block_order, doc_lengths, keys, values)


def fetch_kernel(queries_ref, out_ref, sem):
    copy = pltpu.make_async_copy(queries_ref, out_ref, sem)
    copy.start()
    copy.wait()


def fetch(queries):
    return pl.pallas_call(
        fetch_kernel,
        out_shape=pltpu.VMEM(queries.shape, queries.dtype),
        in_specs=[ANY],
        out_specs=VMEM,
        scratch_shapes=[pltpu.SemaphoreType.DMA],
        cost_estimate=pl.CostEstimate(
            flops=0, transcendentals=0, bytes_accessed=16 * queries.size
        ),
        name="fetch",
    )(queries)


def attend_kernel(count, first, last, span_ref, queries_ref, *refs):
    rows = queries_ref.shape[0]
    half = KH * rows
    columns = GROUP * HD
    part_refs, refs = refs[:count], refs[count:]
    if not first:
        (top_in, total_in, mixed_in), refs = refs[:3], refs[3:]
    if last:
        out_ref, staged, sems = refs
    else:
        top_out, total_out, mixed_out = refs

    lane = lax.broadcasted_iota(jnp.int32, (TAG, HD), 1)
    masks = []
    for early, late in zip(part_refs[::2], part_refs[1::2]):
        block = jnp.where(
            lane < rows,
            early[2 * half :, :].astype(jnp.float32),
            late[2 * half :, :].astype(jnp.float32),
        ).astype(jnp.int32)
        position = (block * BLOCK + lane % BLOCK)[:1, :]
        allowed = (position >= span_ref[0]) & (position <= span_ref[1])
        masks.append(jnp.where(allowed, 0.0, NEGATIVE))
    mask = jnp.concatenate([jnp.concatenate(masks, axis=1)] * GROUP, axis=0)

    scores = []
    for head in range(KH):
        at = head * columns
        queries = jnp.concatenate(
            [queries_ref[:, at + g * HD : at + (g + 1) * HD] for g in range(GROUP)], axis=0
        )
        keys = jnp.concatenate(
            [part[head * rows : (head + 1) * rows, :] for part in part_refs], axis=0
        )
        scores.append(
            lax.dot_general(
                queries, keys, (((1,), (1,)), ((), ())), preferred_element_type=jnp.float32
            )
            + mask
        )
    tops, weights, totals = [], [], []
    for head in range(KH):
        top = jnp.max(scores[head], axis=1, keepdims=True)
        if not first:
            top = jnp.maximum(top, top_in[head])
            wide = jnp.concatenate([top] * len(masks), axis=1)
            weight = jnp.exp2((scores[head] - wide) * SCALE)
        else:
            weight = jnp.exp2((scores[head] - top) * SCALE)
        tops.append(top)
        totals.append(jnp.sum(weight, axis=1, keepdims=True))
        weights.append(weight.astype(jnp.bfloat16))
    copies = []
    for head in range(KH):
        values = jnp.concatenate(
            [part[half + head * rows : half + (head + 1) * rows, :] for part in part_refs],
            axis=0,
        )
        mixed = jnp.dot(weights[head], values, preferred_element_type=jnp.float32)
        total = totals[head]
        if not first:
            factor = jnp.exp2((top_in[head] - tops[head]) * SCALE)
            total = total + total_in[head] * factor
            mixed = mixed + mixed_in[head] * factor
        if not last:
            top_out[head] = jnp.broadcast_to(tops[head], (GROUP * rows, HD))
            total_out[head] = jnp.broadcast_to(total, (GROUP * rows, HD))
            mixed_out[head] = mixed
            continue
        mixed = (mixed * (1.0 / total)).astype(jnp.bfloat16)
        at = head * columns
        for g in range(GROUP):
            staged[:, at + g * HD : at + (g + 1) * HD] = mixed[g * rows : (g + 1) * rows, :]
        here = pl.ds(at, columns)
        copies.append(
            pltpu.make_async_copy(staged.at[:, here], out_ref.at[:, here], sems.at[head])
        )
        copies[head].start()
    for copy in copies:
        copy.wait()


def attend(span, queries, parts, state, last):
    rows = queries.shape[0]
    work = KH * GROUP * rows * len(parts) * rows
    out_shape = (pltpu.VMEM((KH, GROUP * rows, HD), jnp.float32),) * 3
    scratch = []
    if last:
        out_shape = jax.ShapeDtypeStruct(queries.shape, jnp.bfloat16)
        scratch = [pltpu.VMEM(queries.shape, jnp.bfloat16), pltpu.SemaphoreType.DMA((KH,))]
    return pl.pallas_call(
        partial(attend_kernel, len(parts), not state, last),
        out_shape=out_shape,
        in_specs=[VMEM] * (2 + len(parts) + len(state)),
        out_specs=ANY if last else (VMEM, VMEM, VMEM),
        scratch_shapes=scratch,
        compiler_params=pltpu.CompilerParams(vmem_limit_bytes=40 << 20),
        cost_estimate=pl.CostEstimate(
            flops=4 * work * HD, transcendentals=work, bytes_accessed=4 * work
        ),
        name="finish" if last else "begin",
    )(span, queries, *parts, *state)


def on_device(devices, queries, keys, values, block_order, doc_lengths):
    chips = devices // 2
    other_core = [(i, i ^ 1) for i in range(devices)]
    if chips == 4:
        routes = ROUTES
    elif chips & (chips - 1) == 0:
        routes = [[[chip ^ step for chip in range(chips)]] * 2 for step in range(1, chips)]
    else:
        routes = [
            [[(chip + step) % chips for chip in range(chips)]] * 2 for step in range(1, chips)
        ]

    def along(array, route):
        pairs = [
            (2 * chip + core, 2 * route[core][chip] + core)
            for chip in range(chips)
            for core in range(2)
        ]
        return lax.ppermute(array, "ctx", pairs)

    def across(array):
        return lax.ppermute(array, "ctx", other_core)

    own, span = pack(block_order, doc_lengths, keys, values)
    rows = fetch(queries)
    early = [own, across(own)]
    late = []
    for index, route in enumerate(routes):
        part = along(own, route)
        if index == 0:
            rows, part = lax.optimization_barrier((rows, part))
        early.append(part)
        late.append(across(part))
    state = attend(span, rows, early + late[: len(late) % 2], (), False)
    return attend(span, rows, late[len(late) % 2 :], state, True)


ROUTES = (((1, 3, 0, 2), (3, 2, 0, 1)), ((2, 0, 3, 1), (2, 3, 1, 0)), ((3, 2, 1, 0), (1, 0, 3, 2)))


def solution(mesh):
    return jax.shard_map(
        partial(on_device, mesh.shape["ctx"]),
        mesh=mesh,
        in_specs=(
            P(("dp", "ctx"), None),
            P(("dp", "ctx"), None),
            P(("dp", "ctx"), None),
            P(("dp", "ctx")),
            P("dp"),
        ),
        out_specs=P(("dp", "ctx"), None),
        check_vma=False,
    )
```

```python
import math
from functools import partial

import jax
import jax.numpy as jnp
from jax import lax
from jax.experimental import pallas as pl
from jax.experimental.pallas import tpu as pltpu
from jax.sharding import PartitionSpec as P

QH = 16
KH = 4
HD = 128
BLOCK = 32
GROUP = QH // KH
TAG = 8
NEGATIVE = -1e30
SCALE = math.log2(math.e) / math.sqrt(HD)
VMEM = pl.BlockSpec(memory_space=pltpu.VMEM)
ANY = pl.BlockSpec(memory_space=pl.ANY)


def pack_kernel(
    order_ref, lengths_ref, keys_ref, values_ref,
    packed_ref, span_ref, order, lengths, sems,
):
    rows = keys_ref.shape[0]
    half = KH * rows
    copies = [
        pltpu.make_async_copy(order_ref, order, sems.at[0]),
        pltpu.make_async_copy(lengths_ref, lengths, sems.at[1]),
    ]
    for head in range(KH):
        for source, first in ((keys_ref, 0), (values_ref, half)):
            copies.append(
                pltpu.make_async_copy(
                    source.at[:, pl.ds(head * HD, HD)],
                    packed_ref.at[pl.ds(first + head * rows, rows), :],
                    sems.at[len(copies)],
                )
            )
    for copy in copies:
        copy.start()
    copies[0].wait()
    copies[1].wait()
    lane = lax.broadcasted_iota(jnp.int32, (TAG, HD), 1)
    block = jnp.where((lane // BLOCK) % 2 == 0, order[0], order[1])
    packed_ref[2 * half :, :] = block.astype(jnp.float32).astype(jnp.bfloat16)
    row = lax.broadcasted_iota(jnp.int32, (rows, HD), 0)
    position = jnp.where(row < BLOCK, order[0], order[1]) * BLOCK + row % BLOCK
    first = jnp.zeros_like(position)
    end = 0
    for doc in range(lengths.shape[0]):
        end = end + lengths[doc]
        first = jnp.where(position >= end, end, first)
    span_ref[0] = first
    span_ref[1] = position
    for copy in copies[2:]:
        copy.wait()


def pack(block_order, doc_lengths, keys, values):
    rows = keys.shape[0]
    half = KH * rows
    return pl.pallas_call(
        pack_kernel,
        out_shape=(
            pltpu.VMEM((2 * half + TAG, HD), keys.dtype),
            pltpu.VMEM((2, rows, HD), jnp.int32),
        ),
        in_specs=[ANY, ANY, ANY, ANY],
        out_specs=(VMEM, VMEM),
        scratch_shapes=[
            pltpu.SMEM(block_order.shape, jnp.int32),
            pltpu.SMEM(doc_lengths.shape, jnp.int32),
            pltpu.SemaphoreType.DMA((2 + 2 * KH,)),
        ],
        name="pack",
    )(block_order, doc_lengths, keys, values)


def fetch_kernel(queries_ref, out_ref, sem):
    copy = pltpu.make_async_copy(queries_ref, out_ref, sem)
    copy.start()
    copy.wait()


def fetch(queries):
    return pl.pallas_call(
        fetch_kernel,
        out_shape=pltpu.VMEM(queries.shape, queries.dtype),
        in_specs=[ANY],
        out_specs=VMEM,
        scratch_shapes=[pltpu.SemaphoreType.DMA],
        cost_estimate=pl.CostEstimate(
            flops=0, transcendentals=0, bytes_accessed=16 * queries.size
        ),
        name="fetch",
    )(queries)


def attend_kernel(count, first, last, span_ref, queries_ref, *refs):
    rows = queries_ref.shape[0]
    half = KH * rows
    columns = GROUP * HD
    part_refs, refs = refs[:count], refs[count:]
    if not first:
        (top_in, total_in, mixed_in), refs = refs[:3], refs[3:]
    if last:
        out_ref, staged, sems = refs
    else:
        top_out, total_out, mixed_out = refs

    lane = lax.broadcasted_iota(jnp.int32, (TAG, HD), 1)
    masks = []
    for early, late in zip(part_refs[::2], part_refs[1::2]):
        block = jnp.where(
            lane < rows,
            early[2 * half :, :].astype(jnp.float32),
            late[2 * half :, :].astype(jnp.float32),
        ).astype(jnp.int32)
        position = (block * BLOCK + lane % BLOCK)[:1, :]
        allowed = (position >= span_ref[0]) & (position <= span_ref[1])
        masks.append(jnp.where(allowed, 0.0, NEGATIVE))
    mask = jnp.concatenate([jnp.concatenate(masks, axis=1)] * GROUP, axis=0)

    scores = []
    for head in range(KH):
        at = head * columns
        queries = jnp.concatenate(
            [queries_ref[:, at + g * HD : at + (g + 1) * HD] for g in range(GROUP)], axis=0
        )
        keys = jnp.concatenate(
            [part[head * rows : (head + 1) * rows, :] for part in part_refs], axis=0
        )
        scores.append(
            lax.dot_general(
                queries, keys, (((1,), (1,)), ((), ())), preferred_element_type=jnp.float32
            )
            + mask
        )
    tops, weights, totals = [], [], []
    for head in range(KH):
        top = jnp.max(scores[head], axis=1, keepdims=True)
        if not first:
            top = jnp.maximum(top, top_in[head])
            wide = jnp.concatenate([top] * len(masks), axis=1)
            weight = jnp.exp2((scores[head] - wide) * SCALE)
        else:
            weight = jnp.exp2((scores[head] - top) * SCALE)
        tops.append(top)
        totals.append(jnp.sum(weight, axis=1, keepdims=True))
        weights.append(weight.astype(jnp.bfloat16))
    copies = []
    for head in range(KH):
        values = jnp.concatenate(
            [part[half + head * rows : half + (head + 1) * rows, :] for part in part_refs],
            axis=0,
        )
        mixed = jnp.dot(weights[head], values, preferred_element_type=jnp.float32)
        total = totals[head]
        if not first:
            factor = jnp.exp2((top_in[head] - tops[head]) * SCALE)
            total = total + total_in[head] * factor
            mixed = mixed + mixed_in[head] * factor
        if not last:
            top_out[head] = jnp.broadcast_to(tops[head], (GROUP * rows, HD))
            total_out[head] = jnp.broadcast_to(total, (GROUP * rows, HD))
            mixed_out[head] = mixed
            continue
        mixed = (mixed * (1.0 / total)).astype(jnp.bfloat16)
        at = head * columns
        for g in range(GROUP):
            staged[:, at + g * HD : at + (g + 1) * HD] = mixed[g * rows : (g + 1) * rows, :]
        here = pl.ds(at, columns)
        copies.append(
            pltpu.make_async_copy(staged.at[:, here], out_ref.at[:, here], sems.at[head])
        )
        copies[head].start()
    for copy in copies:
        copy.wait()


def attend(span, queries, parts, state, last):
    rows = queries.shape[0]
    work = KH * GROUP * rows * len(parts) * rows
    out_shape = (pltpu.VMEM((KH, GROUP * rows, HD), jnp.float32),) * 3
    scratch = []
    if last:
        out_shape = jax.ShapeDtypeStruct(queries.shape, jnp.bfloat16)
        scratch = [pltpu.VMEM(queries.shape, jnp.bfloat16), pltpu.SemaphoreType.DMA((KH,))]
    return pl.pallas_call(
        partial(attend_kernel, len(parts), not state, last),
        out_shape=out_shape,
        in_specs=[VMEM] * (2 + len(parts) + len(state)),
        out_specs=ANY if last else (VMEM, VMEM, VMEM),
        scratch_shapes=scratch,
        compiler_params=pltpu.CompilerParams(vmem_limit_bytes=40 << 20),
        cost_estimate=pl.CostEstimate(
            flops=4 * work * HD, transcendentals=work, bytes_accessed=4 * work
        ),
        name="finish" if last else "begin",
    )(span, queries, *parts, *state)


def on_device(devices, queries, keys, values, block_order, doc_lengths):
    chips = devices // 2
    other_core = [(i, i ^ 1) for i in range(devices)]
    if chips == 4:
        routes = ROUTES
    elif chips & (chips - 1) == 0:
        routes = [[[chip ^ step for chip in range(chips)]] * 2 for step in range(1, chips)]
    else:
        routes = [
            [[(chip + step) % chips for chip in range(chips)]] * 2 for step in range(1, chips)
        ]

    def along(array, route):
        pairs = [
            (2 * chip + core, 2 * route[core][chip] + core)
            for chip in range(chips)
            for core in range(2)
        ]
        return lax.ppermute(array, "ctx", pairs)

    def across(array):
        return lax.ppermute(array, "ctx", other_core)

    own, span = pack(block_order, doc_lengths, keys, values)
    rows = fetch(queries)
    early = [own, across(own)]
    late = []
    for index, route in enumerate(routes):
        part = along(own, route)
        if index == 0:
            rows, part = lax.optimization_barrier((rows, part))
        early.append(part)
        late.append(across(part))
    state = attend(span, rows, early + late[: len(late) % 2], (), False)
    return attend(span, rows, late[len(late) % 2 :], state, True)


ROUTES = (((2, 3, 0, 1), (3, 2, 0, 1)), ((1, 2, 3, 0), (2, 3, 1, 0)), ((3, 0, 1, 2), (1, 0, 3, 2)))


def solution(mesh):
    return jax.shard_map(
        partial(on_device, mesh.shape["ctx"]),
        mesh=mesh,
        in_specs=(
            P(("dp", "ctx"), None),
            P(("dp", "ctx"), None),
            P(("dp", "ctx"), None),
            P(("dp", "ctx")),
            P("dp"),
        ),
        out_specs=P(("dp", "ctx"), None),
        check_vma=False,
    )
```

```python
import math
from functools import partial

import jax
import jax.numpy as jnp
from jax import lax
from jax.experimental import pallas as pl
from jax.experimental.pallas import tpu as pltpu
from jax.sharding import PartitionSpec as P

QH = 16
KH = 4
HD = 128
BLOCK = 32
GROUP = QH // KH
TAG = 8
NEGATIVE = -1e30
SCALE = math.log2(math.e) / math.sqrt(HD)
VMEM = pl.BlockSpec(memory_space=pltpu.VMEM)
ANY = pl.BlockSpec(memory_space=pl.ANY)


def pack_kernel(
    order_ref, lengths_ref, keys_ref, values_ref,
    packed_ref, span_ref, order, lengths, sems,
):
    rows = keys_ref.shape[0]
    half = KH * rows
    copies = [
        pltpu.make_async_copy(order_ref, order, sems.at[0]),
        pltpu.make_async_copy(lengths_ref, lengths, sems.at[1]),
    ]
    for head in range(KH):
        for source, first in ((keys_ref, 0), (values_ref, half)):
            copies.append(
                pltpu.make_async_copy(
                    source.at[:, pl.ds(head * HD, HD)],
                    packed_ref.at[pl.ds(first + head * rows, rows), :],
                    sems.at[len(copies)],
                )
            )
    for copy in copies:
        copy.start()
    copies[0].wait()
    copies[1].wait()
    lane = lax.broadcasted_iota(jnp.int32, (TAG, HD), 1)
    block = jnp.where((lane // BLOCK) % 2 == 0, order[0], order[1])
    packed_ref[2 * half :, :] = block.astype(jnp.float32).astype(jnp.bfloat16)
    row = lax.broadcasted_iota(jnp.int32, (rows, HD), 0)
    position = jnp.where(row < BLOCK, order[0], order[1]) * BLOCK + row % BLOCK
    first = jnp.zeros_like(position)
    end = 0
    for doc in range(lengths.shape[0]):
        end = end + lengths[doc]
        first = jnp.where(position >= end, end, first)
    span_ref[0] = first
    span_ref[1] = position
    for copy in copies[2:]:
        copy.wait()


def pack(block_order, doc_lengths, keys, values):
    rows = keys.shape[0]
    half = KH * rows
    return pl.pallas_call(
        pack_kernel,
        out_shape=(
            pltpu.VMEM((2 * half + TAG, HD), keys.dtype),
            pltpu.VMEM((2, rows, HD), jnp.int32),
        ),
        in_specs=[ANY, ANY, ANY, ANY],
        out_specs=(VMEM, VMEM),
        scratch_shapes=[
            pltpu.SMEM(block_order.shape, jnp.int32),
            pltpu.SMEM(doc_lengths.shape, jnp.int32),
            pltpu.SemaphoreType.DMA((2 + 2 * KH,)),
        ],
        name="pack",
    )(block_order, doc_lengths, keys, values)


def fetch_kernel(queries_ref, out_ref, sem):
    copy = pltpu.make_async_copy(queries_ref, out_ref, sem)
    copy.start()
    copy.wait()


def fetch(queries):
    return pl.pallas_call(
        fetch_kernel,
        out_shape=pltpu.VMEM(queries.shape, queries.dtype),
        in_specs=[ANY],
        out_specs=VMEM,
        scratch_shapes=[pltpu.SemaphoreType.DMA],
        cost_estimate=pl.CostEstimate(
            flops=0, transcendentals=0, bytes_accessed=16 * queries.size
        ),
        name="fetch",
    )(queries)


def attend_kernel(count, first, last, span_ref, queries_ref, *refs):
    rows = queries_ref.shape[0]
    half = KH * rows
    columns = GROUP * HD
    part_refs, refs = refs[:count], refs[count:]
    if not first:
        (top_in, total_in, mixed_in), refs = refs[:3], refs[3:]
    if last:
        out_ref, staged, sems = refs
    else:
        top_out, total_out, mixed_out = refs

    lane = lax.broadcasted_iota(jnp.int32, (TAG, HD), 1)
    masks = []
    for early, late in zip(part_refs[::2], part_refs[1::2]):
        block = jnp.where(
            lane < rows,
            early[2 * half :, :].astype(jnp.float32),
            late[2 * half :, :].astype(jnp.float32),
        ).astype(jnp.int32)
        position = (block * BLOCK + lane % BLOCK)[:1, :]
        allowed = (position >= span_ref[0]) & (position <= span_ref[1])
        masks.append(jnp.where(allowed, 0.0, NEGATIVE))
    mask = jnp.concatenate([jnp.concatenate(masks, axis=1)] * GROUP, axis=0)

    scores = []
    for head in range(KH):
        at = head * columns
        queries = jnp.concatenate(
            [queries_ref[:, at + g * HD : at + (g + 1) * HD] for g in range(GROUP)], axis=0
        )
        keys = jnp.concatenate(
            [part[head * rows : (head + 1) * rows, :] for part in part_refs], axis=0
        )
        scores.append(
            lax.dot_general(
                queries, keys, (((1,), (1,)), ((), ())), preferred_element_type=jnp.float32
            )
            + mask
        )
    tops, weights, totals = [], [], []
    for head in range(KH):
        top = jnp.max(scores[head], axis=1, keepdims=True)
        if not first:
            top = jnp.maximum(top, top_in[head])
            wide = jnp.concatenate([top] * len(masks), axis=1)
            weight = jnp.exp2((scores[head] - wide) * SCALE)
        else:
            weight = jnp.exp2((scores[head] - top) * SCALE)
        tops.append(top)
        totals.append(jnp.sum(weight, axis=1, keepdims=True))
        weights.append(weight.astype(jnp.bfloat16))
    copies = []
    for head in range(KH):
        values = jnp.concatenate(
            [part[half + head * rows : half + (head + 1) * rows, :] for part in part_refs],
            axis=0,
        )
        mixed = jnp.dot(weights[head], values, preferred_element_type=jnp.float32)
        total = totals[head]
        if not first:
            factor = jnp.exp2((top_in[head] - tops[head]) * SCALE)
            total = total + total_in[head] * factor
            mixed = mixed + mixed_in[head] * factor
        if not last:
            top_out[head] = jnp.broadcast_to(tops[head], (GROUP * rows, HD))
            total_out[head] = jnp.broadcast_to(total, (GROUP * rows, HD))
            mixed_out[head] = mixed
            continue
        mixed = (mixed * (1.0 / total)).astype(jnp.bfloat16)
        at = head * columns
        for g in range(GROUP):
            staged[:, at + g * HD : at + (g + 1) * HD] = mixed[g * rows : (g + 1) * rows, :]
        here = pl.ds(at, columns)
        copies.append(
            pltpu.make_async_copy(staged.at[:, here], out_ref.at[:, here], sems.at[head])
        )
        copies[head].start()
    for copy in copies:
        copy.wait()


def attend(span, queries, parts, state, last):
    rows = queries.shape[0]
    work = KH * GROUP * rows * len(parts) * rows
    out_shape = (pltpu.VMEM((KH, GROUP * rows, HD), jnp.float32),) * 3
    scratch = []
    if last:
        out_shape = jax.ShapeDtypeStruct(queries.shape, jnp.bfloat16)
        scratch = [pltpu.VMEM(queries.shape, jnp.bfloat16), pltpu.SemaphoreType.DMA((KH,))]
    return pl.pallas_call(
        partial(attend_kernel, len(parts), not state, last),
        out_shape=out_shape,
        in_specs=[VMEM] * (2 + len(parts) + len(state)),
        out_specs=ANY if last else (VMEM, VMEM, VMEM),
        scratch_shapes=scratch,
        compiler_params=pltpu.CompilerParams(vmem_limit_bytes=40 << 20),
        cost_estimate=pl.CostEstimate(
            flops=4 * work * HD, transcendentals=work, bytes_accessed=4 * work
        ),
        name="finish" if last else "begin",
    )(span, queries, *parts, *state)


def on_device(devices, queries, keys, values, block_order, doc_lengths):
    chips = devices // 2
    other_core = [(i, i ^ 1) for i in range(devices)]
    if chips == 4:
        routes = ROUTES
    elif chips & (chips - 1) == 0:
        routes = [[[chip ^ step for chip in range(chips)]] * 2 for step in range(1, chips)]
    else:
        routes = [
            [[(chip + step) % chips for chip in range(chips)]] * 2 for step in range(1, chips)
        ]

    def along(array, route):
        pairs = [
            (2 * chip + core, 2 * route[core][chip] + core)
            for chip in range(chips)
            for core in range(2)
        ]
        return lax.ppermute(array, "ctx", pairs)

    def across(array):
        return lax.ppermute(array, "ctx", other_core)

    own, span = pack(block_order, doc_lengths, keys, values)
    rows = fetch(queries)
    early = [own, across(own)]
    late = []
    for index, route in enumerate(routes):
        part = along(own, route)
        if index == 0:
            rows, part = lax.optimization_barrier((rows, part))
        early.append(part)
        late.append(across(part))
    state = attend(span, rows, early + late[: len(late) % 2], (), False)
    return attend(span, rows, late[len(late) % 2 :], state, True)


ROUTES = (((1, 2, 3, 0), (3, 2, 0, 1)), ((2, 3, 0, 1), (1, 0, 3, 2)), ((3, 0, 1, 2), (2, 3, 1, 0)))


def solution(mesh):
    return jax.shard_map(
        partial(on_device, mesh.shape["ctx"]),
        mesh=mesh,
        in_specs=(
            P(("dp", "ctx"), None),
            P(("dp", "ctx"), None),
            P(("dp", "ctx"), None),
            P(("dp", "ctx")),
            P("dp"),
        ),
        out_specs=P(("dp", "ctx"), None),
        check_vma=False,
    )
```
